512 devices in a mesh: gx: 128 (over z, y, core), gy: 4 (over x).
Axes of the slice: x: 4, y: 4, z: 16, core: 2. Of those that a mesh axis runs over, the one named last changes fastest.
Arguments:
- right_side: float32 [12, 2048, 8192], P(None, 'gx', 'gy'), may hold values from -6 to 6
- diffusion: float32 [2048, 8192], P('gx', 'gy'), may hold values from 0.5 to 2
- drift_field: float32 [2, 2048, 8192], P(None, 'gx', 'gy'), may hold values from -3 to 3
- shifts: float32 [6, 2], replicated, may hold values from 1 to 4
Outputs:
- solution: float32 [12, 2048, 8192], P(None, 'gx', 'gy')
The draws below stay inside these ranges and needn't reach their ends.
All inputs are finite; a program needn't handle non-finite values.
Results may differ from the reference program's by a relative error of at most 0.00027.
Values sent between devices are 32-bit elements; how exact they have to be, the bound alone decides.
No kernel may reach another device: no remote copies, remote signals or barrier semaphores. Data moves between devices by JAX's collectives and lax.ppermute only.
A program may use at most 64 MiB of HBM per device.

```python
import math
import jax
import jax.numpy as jnp
import numpy as np
from jax import lax

S = 4
CHANNELS = 12
NX = 2048
NY = 8192


def draw_right_side(key, part):
    base = jax.random.fold_in(key, 7717)
    own_key, common_key, weight_key, sign_key = jax.random.split(base, 4)
    magnitude = jax.random.uniform(weight_key, (CHANNELS,), jnp.float32, 0.5, 1.0)
    signs = jnp.where(jax.random.uniform(sign_key, (CHANNELS,), jnp.float32) < 0.5, -1.0, 1.0)
    weights = (magnitude * signs)[:, None, None]
    own = jax.random.normal(own_key, (CHANNELS, NX, NY), jnp.float32)
    common = jax.random.normal(common_key, (NX, NY), jnp.float32)
    return jnp.clip(0.7 * own + 0.7 * weights * common[None], -6.0, 6.0)


def block_scale(stream_key, extent, cuts, low, top_value):
    def one(dim, shards_of):
        steps = jax.random.uniform(jax.random.fold_in(jax.random.fold_in(stream_key, 6), dim), (shards_of,), jnp.float32, low / len(cuts), top_value / len(cuts))
        return jnp.repeat(jnp.exp(steps), extent[dim] // shards_of).reshape((-1,) + (1,) * (len(extent) - dim - 1))

    factor_of = one(*cuts[0])
    for cut in cuts[1:]:
        factor_of = factor_of * one(*cut)
    return factor_of


def normal_values(rng, dims, deviation, bound, cuts=(), held_as=jnp.bfloat16):
    drawn = deviation * jax.random.normal(rng, dims, jnp.float32)
    if cuts:
        drawn = drawn * block_scale(rng, dims, cuts, -0.22, 0.18)
    return jnp.clip(drawn, -bound, bound).astype(held_as)


def setup_inputs(seed: int = 0) -> dict:
    seeds = jax.random.split(jax.random.key(seed), 5)
    return {
        "right_side": draw_right_side(jax.random.fold_in(seeds[4], 71), 0),
        "diffusion": jnp.clip(jnp.exp(math.log(2.0) - 1.3862944 * jax.random.uniform(seeds[1], (NX, NY), jnp.float32) ** block_scale(seeds[1], (NX, NY), ((0, 128), (1, 4)), -0.2, 0.2)), 0.5, 2.0),
        "drift_field": normal_values(seeds[2], (2, NX, NY), 0.5, 3.0, ((1, 128), (2, 4)), jnp.float32),
        "shifts": jnp.clip(jax.random.uniform(seeds[3], (6, 2), jnp.float32, 1.0, 4.0), 1.0, 4.0),
    }


newton_shifts = (-8.0, -2.0, -14.0, -5.0)
newton_scale = 8.0
highest = lax.Precision.HIGHEST

def generator(padded, diffusion, drift_field):
    center = padded[:, 1:-1, 1:-1]
    forward_x = padded[:, 2:, 1:-1]
    backward_x = padded[:, :-2, 1:-1]
    forward_y = padded[:, 1:-1, 2:]
    backward_y = padded[:, 1:-1, :-2]
    spread_term = diffusion * (forward_x + backward_x + forward_y + backward_y - 4.0 * center)
    return spread_term + 0.5 * drift_field[0] * (forward_x - backward_x) + 0.5 * drift_field[1] * (forward_y - backward_y)

def newton_step(padded, diffusion, drift_field, degree):
    center = padded[:, 1:-1, 1:-1]
    return (generator(padded, diffusion, drift_field) - newton_shifts[degree] * center) / newton_scale

def change_matrix(channels, degrees):
    change_table = np.zeros(((degrees + 1) * channels, degrees * channels), np.float32)
    for degree in range(degrees):
        for component in range(channels):
            column = degree * channels + component
            change_table[column, column] = newton_shifts[degree]
            change_table[column + channels, column] = newton_scale
    return change_table

def solve_shifts(upper_factor, shifts):
    channels = 2 * shifts.shape[0]
    columns = upper_factor.shape[1] - channels
    change = jnp.asarray(change_matrix(channels, columns // channels))
    select = jnp.asarray(np.eye(upper_factor.shape[0], columns, dtype=np.float32))

    def single(shift_index):
        shift_real = shifts[shift_index, 0]
        shift_imag = shifts[shift_index, 1]
        real_part = jnp.dot(upper_factor, change - shift_real * select, precision=highest)
        imag_part = -shift_imag * upper_factor[:, :columns]
        system = jnp.concatenate([jnp.concatenate([real_part, -imag_part], axis=1), jnp.concatenate([imag_part, real_part], axis=1)], axis=0)
        target = jnp.concatenate([upper_factor[:, 2 * shift_index], upper_factor[:, 2 * shift_index + 1]])
        normal = jnp.dot(system.T, system, precision=highest)
        moment = jnp.dot(system.T, target, precision=highest)[:, None]
        factor = jnp.linalg.cholesky(normal)
        middle = lax.linalg.triangular_solve(factor, moment, left_side=True, lower=True)
        answer = lax.linalg.triangular_solve(factor, middle, left_side=True, lower=True, transpose_a=True)
        answer = answer[:, 0]
        return (answer[:columns], answer[columns:])
    real_parts, imag_parts = jax.vmap(single)(jnp.arange(shifts.shape[0]))
    return jnp.stack([real_parts, imag_parts], axis=1).reshape(channels, columns)

def pad_grid(field):
    wrapped = jnp.concatenate([field[:, -1:], field, field[:, :1]], axis=1)
    return jnp.pad(wrapped, ((0, 0), (0, 0), (1, 1)))

def reference(right_side, diffusion, drift_field, shifts):
    krylov = [right_side]
    for degree in range(S):
        krylov.append(newton_step(pad_grid(krylov[-1]), diffusion, drift_field, degree))
    block_rows = []
    for left_index in range(S + 1):
        block_row = []
        for right_index in range(S + 1):
            block_row.append(jnp.einsum('axy,bxy->ab', krylov[left_index], krylov[right_index], precision=highest))
        block_rows.append(jnp.concatenate(block_row, axis=1))
    global_gram = jnp.concatenate(block_rows, axis=0)
    upper_factor = jnp.linalg.cholesky(global_gram).T
    mixing = solve_shifts(upper_factor, shifts)
    solution = jnp.zeros_like(right_side)
    for degree in range(S):
        part_mix = mixing[:, degree * CHANNELS:(degree + 1) * CHANNELS]
        solution = solution + jnp.einsum('ac,cxy->axy', part_mix, krylov[degree], precision=highest)
    return solution
```

```python
import functools

import jax
import jax.numpy as jnp
import numpy as np
from jax import lax
from jax.experimental import pallas as pl
from jax.experimental.pallas import tpu as pltpu
from jax.sharding import Mesh
from jax.sharding import PartitionSpec as P

S = 4
THETA = (-8.0, -2.0, -14.0, -5.0)
SCALE = 8.0
CH = 12
HALO = 4
LANE = 128
HIGH = lax.Precision.HIGHEST
F32 = jnp.float32
BF16 = jnp.bfloat16
HI_AT = (0, 16, 32, 48, 128)
LO_AT = (64, 80, 96, 112, 144)
ROWS = 160


def selection():
    pick = np.zeros((64, ROWS), np.float32)
    for k in range(S + 1):
        for c in range(CH):
            i = k * CH + c
            at = i if i < 30 else i + 2
            pick[at, HI_AT[k] + c] = 1.0
            pick[at, LO_AT[k] + c] = 1.0
    return pick


def expansion():
    spread = np.zeros((64, 48), np.float32)
    for k in range(S):
        for c in range(CH):
            spread[k * 16 + c, k * CH + c] = 1.0
    return spread


def split(value):
    high = value.astype(BF16)
    return high, (value - high.astype(F32)).astype(BF16)


def krylov_kernel(own, low, high, side, pick, basis, gram, va, vb, coef, acc, *, tile_rows, tile_cols):
    wide = tile_cols + LANE
    depth = tile_rows + 2 * HALO

    def load(r, src, at):
        va[r, :, :, :tile_cols] = src[at]
        va[r, :, :, tile_cols:] = side[r]

    def fill_low(i, _):
        load(i, low, i)
        return 0

    def fill_high(i, _):
        load(i + HALO + tile_rows, high, i)
        return 0

    def keep(k, r, value):
        hi, lo = split(value[:, :, :tile_cols].reshape(16, tile_cols))
        basis[r, HI_AT[k] : HI_AT[k] + 16, :] = hi
        basis[r, LO_AT[k] : LO_AT[k] + 16, :] = lo

    def fill_own(i, _):
        load(i + HALO, own, i)
        keep(0, i, own[i])
        return 0

    lax.fori_loop(0, HALO, fill_low, 0)
    lax.fori_loop(0, HALO, fill_high, 0)
    lax.fori_loop(0, tile_rows, fill_own, 0)

    def coefficients(r, _):
        spread = jnp.broadcast_to(va[r, 1, 4:5, :], (8, wide)) * (1.0 / SCALE)
        drift_x = jnp.broadcast_to(va[r, 1, 5:6, :], (8, wide)) * (0.5 / SCALE)
        drift_y = jnp.broadcast_to(va[r, 1, 6:7, :], (8, wide)) * (0.5 / SCALE)
        coef[r, 0] = spread + drift_x
        coef[r, 1] = spread - drift_x
        coef[r, 2] = spread + drift_y
        coef[r, 3] = spread - drift_y
        coef[r, 4] = -4.0 * spread
        return 0

    lax.fori_loop(1, depth - 1, coefficients, 0)

    bufs = (va, vb)
    for k in range(S):
        src, dst = bufs[k % 2], bufs[(k + 1) % 2]

        def advance(r, k=k, src=src, dst=dst):
            center = src[r]
            value = (
                coef[r, 0][None] * src[r + 1]
                + coef[r, 1][None] * src[r - 1]
                + coef[r, 2][None] * pltpu.roll(center, wide - 1, 2)
                + coef[r, 3][None] * pltpu.roll(center, 1, 2)
                + (coef[r, 4] - THETA[k] / SCALE)[None] * center
            )
            if k < S - 1:
                dst[r] = value
            return value

        def outer(r, _, advance=advance):
            advance(r)
            return 0

        def inner(i, _, k=k, advance=advance):
            keep(k + 1, i, advance(i + HALO))
            return 0

        if k < S - 1:
            lax.fori_loop(k + 1, HALO, outer, 0)
            lax.fori_loop(HALO + tile_rows, depth - 1 - k, outer, 0)
        lax.fori_loop(0, tile_rows, inner, 0)

    acc[...] = jnp.zeros_like(acc)

    def accumulate(i, _):
        rows = basis[i]
        acc[...] += lax.dot_general(rows, rows, (((1,), (1,)), ((), ())), preferred_element_type=F32)
        return 0

    lax.fori_loop(0, tile_rows, accumulate, 0)
    half = jnp.dot(pick[...], acc[...], precision=HIGH, preferred_element_type=F32)
    gram[...] = lax.dot_general(half, pick[...], (((1,), (1,)), ((), ())), precision=HIGH, preferred_element_type=F32)


def lane(shape):
    return lax.broadcasted_iota(jnp.int32, shape, len(shape) - 1)


def solve_kernel(shifts, gram, spread, basis_hbm, out, basis, mixed, sem, *, tile_rows, tile_cols):
    copy = pltpu.make_async_copy(basis_hbm.at[:, 0:128, :], basis, sem)
    copy.start()

    g = gram[...]
    lanes = lane((48, 2 * 64))
    theta_col = jnp.zeros((48, 128), F32)
    theta_row = jnp.zeros((48, 128), F32)
    rows_id = lax.broadcasted_iota(jnp.int32, (48, 128), 0)
    for k in range(S):
        theta_row = jnp.where((rows_id >= 12 * k) & (rows_id < 12 * k + 12), THETA[k], theta_row)
        theta_col = jnp.where((lanes >= 12 * k) & (lanes < 12 * k + 12), THETA[k], theta_col)
    g0 = g[0:48]
    gd = pltpu.roll(g, 64 - 12, 0)[0:48]
    gr = pltpu.roll(g0, 128 - 12, 1)
    grd = pltpu.roll(gd, 128 - 12, 1)
    inside = lanes < 48
    at_rhs = lanes == 48
    systems = []
    for j in range(CH // 2):
        a = shifts[j, 0]
        b = shifts[j, 1]
        alpha_i = theta_row - a
        alpha_l = theta_col - a
        real = (alpha_i * alpha_l + b * b) * g0 + SCALE * (alpha_i * gr + alpha_l * gd) + SCALE * SCALE * grd
        imag = b * ((alpha_l - alpha_i) * g0 + SCALE * (gr - gd))
        g1 = pltpu.roll(g0, 48 - 2 * j, 1)
        g2 = pltpu.roll(g0, 47 - 2 * j, 1)
        gd1 = pltpu.roll(gd, 48 - 2 * j, 1)
        gd2 = pltpu.roll(gd, 47 - 2 * j, 1)
        rhs_real = alpha_i * g1 - b * g2 + SCALE * gd1
        rhs_imag = alpha_i * g2 + b * g1 + SCALE * gd2
        real = jnp.where(inside, real, jnp.where(at_rhs, rhs_real, 0.0))
        imag = jnp.where(inside, imag, jnp.where(at_rhs, rhs_imag, 0.0))
        systems.append(real + pltpu.roll(imag, 64, 1))

    flip = jnp.where(lane((1, 128)) < 64, -1.0, 1.0)
    for k in range(48):
        for j in range(CH // 2):
            m = systems[j]
            col_real = jnp.broadcast_to(m[:, k : k + 1], (48, 128))
            col_imag = jnp.broadcast_to(m[:, 64 + k : 65 + k], (48, 128))
            inverse = 1.0 / col_real[k : k + 1, :]
            row = m[k : k + 1, :] * inverse
            turned = pltpu.roll(row, 64, 1) * flip
            pivot = rows_id == k
            update = m - col_real * row - col_imag * turned
            systems[j] = jnp.where(pivot, jnp.broadcast_to(row, (48, 128)), update)

    mix = jnp.zeros((48, 128), F32)
    for j in range(CH // 2):
        m = systems[j]
        mix = jnp.where(lanes == 2 * j, jnp.broadcast_to(m[:, 48:49], (48, 128)), mix)
        mix = jnp.where(lanes == 2 * j + 1, jnp.broadcast_to(m[:, 112:113], (48, 128)), mix)
    mix = jnp.dot(spread[...], mix, precision=HIGH, preferred_element_type=F32)
    mix_hi, mix_lo = split(mix)
    weights = mix_hi.astype(F32) + pltpu.roll(mix_lo.astype(F32), 16, 1)
    weights = jnp.concatenate([weights, weights], axis=0).T[0:32].astype(BF16)

    copy.wait()

    def combine(i, _):
        both = jnp.dot(weights, basis[i], preferred_element_type=F32)
        mixed[i] = both[0:16] + both[16:32]
        return 0

    lax.fori_loop(0, tile_rows, combine, 0)
    out[...] = mixed[:, 0:CH, :]


def per_device(right_side, diffusion, drift_field, shifts):
    tile_rows, tile_cols = right_side.shape[1:]
    fields = jnp.concatenate(
        [right_side, diffusion[None], drift_field, jnp.zeros((1, tile_rows, tile_cols), F32)], axis=0
    )
    fields = fields.transpose(1, 0, 2)
    gx = ("z", "y", "core")
    count = lax.axis_size(gx)
    ring_up = [(i, (i + 1) % count) for i in range(count)]
    ring_down = [(i, (i - 1) % count) for i in range(count)]
    low = lax.ppermute(fields[-HALO:], gx, ring_up)
    high = lax.ppermute(fields[:HALO], gx, ring_down)
    gy = lax.axis_size("x")
    edge_right = jnp.concatenate([p[:, :, -LANE:] for p in (low, fields, high)], axis=0)
    edge_left = jnp.concatenate([p[:, :, :LANE] for p in (low, fields, high)], axis=0)
    from_left = lax.ppermute(edge_right, "x", [(i, i + 1) for i in range(gy - 1)])
    from_right = lax.ppermute(edge_left, "x", [(i + 1, i) for i in range(gy - 1)])
    side = jnp.where(lax.broadcasted_iota(jnp.int32, from_left.shape, 2) < LANE // 2, from_right, from_left)

    def halves(x):
        return x.reshape(x.shape[0], 2, 8, x.shape[2])

    wide, depth = tile_cols + LANE, tile_rows + 2 * HALO
    basis, gram = pl.pallas_call(
        functools.partial(krylov_kernel, tile_rows=tile_rows, tile_cols=tile_cols),
        out_shape=(
            jax.ShapeDtypeStruct((tile_rows, ROWS, tile_cols), BF16),
            jax.ShapeDtypeStruct((64, 64), F32),
        ),
        scratch_shapes=[
            pltpu.VMEM((depth, 2, 8, wide), F32),
            pltpu.VMEM((depth, 2, 8, wide), F32),
            pltpu.VMEM((depth, 5, 8, wide), F32),
            pltpu.VMEM((ROWS, ROWS), F32),
        ],
        compiler_params=pltpu.CompilerParams(vmem_limit_bytes=60 * 2**20),
        name="krylov",
    )(halves(fields), halves(low), halves(high), halves(side), jnp.asarray(selection()))

    first, cross, second = gram[:32, :32], gram[:32, 32:], gram[32:, 32:]
    row = lax.broadcasted_iota(jnp.int32, (32, 32), 0)
    column = lax.broadcasted_iota(jnp.int32, (32, 32), 1)
    packed = jnp.where(row >= column, first, second)
    diagonal = jnp.sum(jnp.where(row == column, second, 0.0), axis=1, keepdims=True)
    packed = jnp.where(column == 31, diagonal, packed)
    payload = jnp.concatenate([cross, packed], axis=1)
    payload = jnp.concatenate([payload[:16], payload[16:]], axis=1)
    for axes in (("y", "core", "x"), ("z",)):
        members = lax.axis_size(axes)
        parts = lax.all_to_all(jnp.broadcast_to(payload[None], (members, 16, LANE)), axes, 0, 0, tiled=True)
        payload = jnp.sum(parts, axis=0)
    payload = jnp.concatenate([payload[:, :64], payload[:, 64:]], axis=0)
    cross, packed = payload[:30, :30], payload[:30, 32:62]
    diagonal = payload[:30, 63]
    row, column = row[:30, :30], column[:30, :30]
    first = jnp.where(row >= column, packed, packed.T)
    second = jnp.where(row < column, packed, packed.T)
    second = jnp.where(row == column, diagonal[None], second)
    gram = jnp.concatenate(
        [jnp.concatenate([first, cross], axis=1), jnp.concatenate([cross.T, second], axis=1)], axis=0
    )
    gram = jnp.pad(gram, ((0, 4), (0, 68)))

    out = pl.pallas_call(
        functools.partial(solve_kernel, tile_rows=tile_rows, tile_cols=tile_cols),
        out_shape=jax.ShapeDtypeStruct((tile_rows, CH, tile_cols), F32),
        in_specs=[
            pl.BlockSpec(memory_space=pltpu.SMEM),
            pl.BlockSpec(memory_space=pltpu.VMEM),
            pl.BlockSpec(memory_space=pltpu.VMEM),
            pl.BlockSpec(memory_space=pl.ANY),
        ],
        scratch_shapes=[
            pltpu.VMEM((tile_rows, 128, tile_cols), BF16),
            pltpu.VMEM((tile_rows, 16, tile_cols), F32),
            pltpu.SemaphoreType.DMA,
        ],
        compiler_params=pltpu.CompilerParams(vmem_limit_bytes=60 * 2**20),
        name="solve",
    )(shifts, gram, jnp.asarray(expansion()), basis)
    return out.transpose(1, 0, 2)


def solution(mesh):
    fine = Mesh(mesh.devices.reshape(16, 4, 2, 4), ("z", "y", "core", "x"))
    gx = ("z", "y", "core")
    in_specs = (P(None, gx, "x"), P(gx, "x"), P(None, gx, "x"), P())
    return jax.shard_map(
        per_device, mesh=fine, in_specs=in_specs, out_specs=P(None, gx, "x"), check_vma=False
    )
```

```python
import jax
import jax.numpy as jnp
import numpy as np
from jax import lax
from jax.experimental import pallas as pl
from jax.experimental.pallas import tpu as pltpu
from jax.sharding import Mesh
from jax.sharding import PartitionSpec as P

S = 4
THETA = (-8.0, -2.0, -14.0, -5.0)
SCALE = 8.0
CH = 12
HALO = 4
LANE = 128
HIGH = lax.Precision.HIGHEST
F32 = jnp.float32
BF16 = jnp.bfloat16
HI_AT = (0, 16, 32, 48, 128)
LO_AT = (64, 80, 96, 112, 144)
ROWS = 160


def selection():
    pick = np.zeros((128, ROWS), np.float32)
    for k in range(S + 1):
        for c in range(CH):
            i = k * CH + c
            at = i if i < 30 else i + 2
            pick[at, HI_AT[k] + c] = 1.0
            pick[at, LO_AT[k] + c] = 1.0
    return pick


def expansion():
    spread = np.zeros((64, 48), np.float32)
    for k in range(S):
        for c in range(CH):
            spread[k * 16 + c, k * CH + c] = 1.0
    return spread


def split(value):
    high = value.astype(BF16)
    return high, (value - high.astype(F32)).astype(BF16)


def coefficients(coef, at, field):
    shape = (8, field.shape[-1])
    spread = jnp.broadcast_to(field[1, 4:5, :], shape) * (1.0 / SCALE)
    drift_x = jnp.broadcast_to(field[1, 5:6, :], shape) * (0.5 / SCALE)
    drift_y = jnp.broadcast_to(field[1, 6:7, :], shape) * (0.5 / SCALE)
    coef[at, 0] = spread + drift_x
    coef[at, 1] = spread - drift_x
    coef[at, 2] = spread + drift_y
    coef[at, 3] = spread - drift_y
    coef[at, 4] = -4.0 * spread


def newton_row(coef, at, k, center, after, before):
    wide = center.shape[-1]
    return (
        coef[at, 0][None] * after
        + coef[at, 1][None] * before
        + coef[at, 2][None] * pltpu.roll(center, wide - 1, 2)
        + coef[at, 3][None] * pltpu.roll(center, 1, 2)
        + (coef[at, 4] - THETA[k] / SCALE)[None] * center
    )


def keep(pieces, at, k, value):
    cols = pieces.shape[-1]
    hi, lo = split(value[:, :, :cols].reshape(16, cols))
    pieces[at, HI_AT[k] : HI_AT[k] + 16, :] = hi
    pieces[at, LO_AT[k] : LO_AT[k] + 16, :] = lo


def add_gram(acc, rows):
    acc[...] += lax.dot_general(rows, rows, (((1,), (1,)), ((), ())), preferred_element_type=F32)


def middle_kernel(own, side, basis, first, second, third, acc, v1, v2, v3, coef, pieces, sems):
    tile_rows = own.shape[0]
    levels = (None, v1, v2, v3)
    acc[...] = jnp.zeros_like(acc)
    copies = []

    def start(source, target):
        copy = pltpu.make_async_copy(source, target, sems.at[len(copies)])
        copy.start()
        copies.append(copy)

    def get(k, r):
        if k:
            return levels[k][r]
        return jnp.concatenate([own[r], side[r]], axis=2)

    for front in range(1, tile_rows + 1):
        if front < tile_rows - 1:
            coefficients(coef, front, get(0, front))
        for k in range(S):
            r = front - k
            if k < r < tile_rows - 1 - k:
                value = newton_row(coef, r, k, get(k, r), get(k, r + 1), get(k, r - 1))
                if k < S - 1:
                    levels[k + 1][r] = value
                    group, at = (first, second, third)[k], export_at(k + 1, r, tile_rows)
                    if at is not None:
                        start(levels[k + 1].at[r], group.at[at])
                if HALO <= r < tile_rows - HALO:
                    keep(pieces, r - HALO, k + 1, value)
                    if k == 0:
                        keep(pieces, r - HALO, 0, get(0, r))
        r = front - S
        if HALO <= r < tile_rows - HALO:
            add_gram(acc, pieces[r - HALO])
            start(pieces.at[r - HALO, 0:128, :], basis.at[r - HALO])
    for copy in copies:
        copy.wait()


def export_at(k, r, tile_rows):
    low = {1: (1, 2, 3), 2: (2, 3), 3: (3, 4)}[k]
    rows = low + tuple(tile_rows - 1 - i for i in reversed(low))
    return rows.index(r) if r in rows else None


def edge_kernel(
    own, side, low, high, first, second, third, middle, pick, basis, payload, v1, v2, v3, coef, pieces, acc, sems
):
    tile_rows = own.shape[0]
    levels = (None, v1, v2, v3)
    exports = (None, first, second, third)
    acc[...] = middle[...]
    copies = []

    def get(k, r):
        if k:
            at = export_at(k, r, tile_rows)
            return levels[k][r + HALO] if at is None else exports[k][at]
        if r < 0:
            return low[r + HALO]
        if r >= tile_rows:
            return high[r - tile_rows]
        return jnp.concatenate([own[r], side[r]], axis=2)

    def finish(at):
        add_gram(acc, pieces[at])
        copy = pltpu.make_async_copy(pieces.at[at, 0:128, :], basis.at[at], sems.at[at])
        copy.start()
        copies.append(copy)

    ready = []
    for far in (False, True):
        def place(i):
            return tile_rows - 1 - i if far else i

        def slot(i):
            return i + HALO if far else i

        for i in range(1 - HALO, HALO):
            coefficients(coef, place(i) + HALO, get(0, place(i)))
        for k in range(S):
            for i in range(k + 1 - HALO, k + 1):
                r = place(i)
                value = newton_row(coef, r + HALO, k, get(k, r), get(k, r + 1), get(k, r - 1))
                if k < S - 1:
                    levels[k + 1][r + HALO] = value
                if i >= 0:
                    keep(pieces, slot(i), k + 1, value)
                if k == S - 1:
                    ready.append(slot(i))
                if ready and (far or k == S - 1) and i % 2 == 1:
                    finish(ready.pop(0))
            for i in range(k + 1, HALO):
                if k < S - 1:
                    keep(pieces, slot(i), k + 1, get(k + 1, place(i)))
            if k == 0:
                for i in range(HALO):
                    keep(pieces, slot(i), 0, get(0, place(i)))
    for at in ready:
        finish(at)

    half = jnp.dot(pick[0:64, :], acc[...], precision=HIGH, preferred_element_type=F32)
    gram = lax.dot_general(half, pick[...], (((1,), (1,)), ((), ())), precision=HIGH, preferred_element_type=F32)
    row = lax.broadcasted_iota(jnp.int32, (32, 128), 0)
    column = lax.broadcasted_iota(jnp.int32, (32, 128), 1)
    one, two = gram[0:32], gram[32:64]
    cross = pltpu.roll(one, 96, 1)
    shifted = pltpu.roll(one, 32, 1)
    diagonal = jnp.sum(jnp.where(column == row + 32, two, 0.0), axis=1, keepdims=True)
    packed = jnp.where(row + 32 >= column, shifted, two)
    packed = jnp.where(column == 63, jnp.broadcast_to(diagonal, (32, 128)), packed)
    whole = jnp.where(column < 32, cross, packed)
    whole = jnp.where(column < 64, whole, 0.0)
    folded = whole[0:16] + pltpu.roll(whole[16:32], 64, 1)
    payload[...] = jnp.broadcast_to(folded[None], payload.shape)
    for copy in copies:
        copy.wait()


def lane(shape):
    return lax.broadcasted_iota(jnp.int32, shape, len(shape) - 1)


def unpack(parts):
    total = parts[0]
    for i in range(1, parts.shape[0]):
        total = total + parts[i]
    row = lax.broadcasted_iota(jnp.int32, (32, 128), 0)
    column = lax.broadcasted_iota(jnp.int32, (32, 128), 1)
    whole = jnp.concatenate([total, pltpu.roll(total, 64, 1)], axis=0)
    whole = jnp.where(column < 64, whole, 0.0)
    flipped = jnp.concatenate([whole, jnp.zeros((96, 128), F32)], axis=0).T
    packed = pltpu.roll(whole, 96, 1)
    turned = flipped[32:64]
    diagonal = jnp.broadcast_to(whole[:, 63:64], (32, 128))
    first = jnp.where(row >= column, packed, turned)
    second = jnp.where(row < column, packed, turned)
    second = jnp.where(row == column, diagonal, second)
    left = column < 32
    top = jnp.where(left, first, pltpu.roll(whole, 32, 1))
    bottom = jnp.where(left, flipped[0:32], pltpu.roll(second, 32, 1))
    gram = jnp.concatenate([top, bottom], axis=0)
    gram = jnp.where(lane((64, 128)) < 30, gram, pltpu.roll(gram, 126, 1))
    return jnp.where(lax.broadcasted_iota(jnp.int32, (64, 128), 0) < 30, gram, pltpu.roll(gram, 62, 0))


def normal_systems(g, shifts):
    lanes = lane((48, 128))
    rows_id = lax.broadcasted_iota(jnp.int32, (48, 128), 0)
    theta_col = jnp.zeros((48, 128), F32)
    theta_row = jnp.zeros((48, 128), F32)
    for k in range(S):
        theta_row = jnp.where((rows_id >= 12 * k) & (rows_id < 12 * k + 12), THETA[k], theta_row)
        theta_col = jnp.where((lanes >= 12 * k) & (lanes < 12 * k + 12), THETA[k], theta_col)
    g0 = g[0:48]
    gd = pltpu.roll(g, 64 - 12, 0)[0:48]
    gr = pltpu.roll(g0, 128 - 12, 1)
    grd = pltpu.roll(gd, 128 - 12, 1)
    inside = lanes < 48
    at_rhs = lanes == 48
    systems = []
    for j in range(CH // 2):
        a = shifts[0, j]
        b = shifts[1, j]
        alpha_i = theta_row - a
        alpha_l = theta_col - a
        real = (alpha_i * alpha_l + b * b) * g0 + SCALE * (alpha_i * gr + alpha_l * gd) + SCALE * SCALE * grd
        imag = b * ((alpha_l - alpha_i) * g0 + SCALE * (gr - gd))
        g1 = pltpu.roll(g0, 48 - 2 * j, 1)
        g2 = pltpu.roll(g0, 47 - 2 * j, 1)
        gd1 = pltpu.roll(gd, 48 - 2 * j, 1)
        gd2 = pltpu.roll(gd, 47 - 2 * j, 1)
        rhs_real = alpha_i * g1 - b * g2 + SCALE * gd1
        rhs_imag = alpha_i * g2 + b * g1 + SCALE * gd2
        real = jnp.where(inside, real, jnp.where(at_rhs, rhs_real, 0.0))
        imag = jnp.where(inside, imag, jnp.where(at_rhs, rhs_imag, 0.0))
        system = real + pltpu.roll(imag, 64, 1)
        systems.append([system[8 * i : 8 * i + 8] for i in range(6)])
    return systems


def column_of(block, at):
    return jnp.broadcast_to(block[:, at : at + 1], (8, 128))


def eliminate(systems):
    flip = jnp.where(lane((1, 128)) < 64, -1.0, 1.0)
    rows_id = lax.broadcasted_iota(jnp.int32, (8, 128), 0)
    for k in range(0, 48, 2):
        at, p = k // 8, k % 8
        for blocks in systems:
            pivot = blocks[at]
            row0, row1 = pivot[p : p + 1], pivot[p + 1 : p + 2]
            turn0 = pltpu.roll(row0, 64, 1) * flip
            turn1 = pltpu.roll(row1, 64, 1) * flip
            columns = [
                [column_of(b, c) for c in (k, 64 + k, k + 1, 65 + k)] for b in blocks
            ]
            c0r, _, c1r, c1i = columns[at]
            a, zr, zi, d = c0r[p : p + 1], c1r[p : p + 1], c1i[p : p + 1], c1r[p + 1 : p + 2]
            scale = 1.0 / (a * d - (zr * zr + zi * zi))
            a, zr, zi, d = a * scale, zr * scale, zi * scale, d * scale
            x0 = d * row0 - (zr * row1 + zi * turn1)
            x1 = a * row1 - (zr * row0 - zi * turn0)
            t0 = d * turn0 - (zr * turn1 - zi * row1)
            t1 = a * turn1 - (zr * turn0 + zi * row0)
            for i in range(6):
                c0r, c0i, c1r, c1i = columns[i]
                update = blocks[i] - ((c0r * x0 + c0i * t0) + (c1r * x1 + c1i * t1))
                if i == at:
                    update = jnp.where(rows_id == p, x0, jnp.where(rows_id == p + 1, x1, update))
                blocks[i] = update
    return systems


def solve_kernel(shifts, parts, spread, middle_hbm, edge_hbm, out, middle, edge, mixed, sems):
    tile_rows = middle.shape[0] + edge.shape[0]
    strips = mixed.shape[0]
    copies = [
        pltpu.make_async_copy(middle_hbm, middle, sems.at[0]),
        pltpu.make_async_copy(edge_hbm, edge, sems.at[1]),
    ]
    for copy in copies:
        copy.start()

    systems = eliminate(normal_systems(unpack(parts), shifts))
    lanes = lane((48, 128))
    mix = jnp.zeros((48, 128), F32)
    for j, blocks in enumerate(systems):
        m = jnp.concatenate(blocks, axis=0)
        mix = jnp.where(lanes == 2 * j, jnp.broadcast_to(m[:, 48:49], (48, 128)), mix)
        mix = jnp.where(lanes == 2 * j + 1, jnp.broadcast_to(m[:, 112:113], (48, 128)), mix)
    mix = jnp.dot(spread[...], mix, precision=HIGH, preferred_element_type=F32)
    mix_hi, mix_lo = split(mix)
    weights = mix_hi.astype(F32) + pltpu.roll(mix_lo.astype(F32), 16, 1)
    weights = jnp.concatenate([weights, weights], axis=0).T[0:32].astype(BF16)

    for copy in copies:
        copy.wait()

    def combine(pieces, r):
        both = jnp.dot(weights, pieces, preferred_element_type=F32)
        both = both[0:16] + both[16:32]
        for j in range(strips):
            mixed.at[j][pl.ds(r, CH, stride=tile_rows), :] = both[0:CH, j * LANE : (j + 1) * LANE]

    for i in range(tile_rows - 2 * HALO):
        combine(middle[i], i + HALO)
    for i in range(HALO):
        combine(edge[i], i)
        combine(edge[i + HALO], tile_rows - 1 - i)
    copies = [
        pltpu.make_async_copy(mixed.at[j], out.at[:, j * LANE : (j + 1) * LANE], sems.at[2 + j]) for j in range(strips)
    ]
    for copy in copies:
        copy.start()
    for copy in copies:
        copy.wait()


def per_device(right_side, diffusion, drift_field, shifts):
    tile_rows, tile_cols = right_side.shape[1:]
    wide, mid_rows, depth = tile_cols + LANE, tile_rows - 2 * HALO, tile_rows + 2 * HALO
    raw = (right_side, diffusion[None], drift_field, jnp.zeros((1, tile_rows, tile_cols), F32))
    gy = lax.axis_size("x")
    from_left = lax.ppermute(
        jnp.concatenate([f[:, :, -LANE:] for f in raw]), "x", [(i, i + 1) for i in range(gy - 1)]
    )
    from_right = lax.ppermute(
        jnp.concatenate([f[:, :, :LANE] for f in raw]), "x", [(i + 1, i) for i in range(gy - 1)]
    )
    side = jnp.where(lax.broadcasted_iota(jnp.int32, from_left.shape, 2) < LANE // 2, from_right, from_left)
    side = side.transpose(1, 0, 2)
    fields = jnp.concatenate(raw, axis=0).transpose(1, 0, 2)
    gx = ("z", "y", "core")
    count = lax.axis_size(gx)
    low = lax.ppermute(
        jnp.concatenate([fields[-HALO:], side[-HALO:]], axis=2), gx, [(i, (i + 1) % count) for i in range(count)]
    )
    high = lax.ppermute(
        jnp.concatenate([fields[:HALO], side[:HALO]], axis=2), gx, [(i, (i - 1) % count) for i in range(count)]
    )

    def halves(x):
        return x.reshape(x.shape[0], 2, 8, x.shape[2])

    def rows_of(n, width=wide):
        return (n, 2, 8, width)

    fields, side, low, high = halves(fields), halves(side), halves(low), halves(high)
    anywhere = pl.BlockSpec(memory_space=pl.ANY)
    vmem = pl.BlockSpec(memory_space=pltpu.VMEM)
    params = pltpu.CompilerParams(vmem_limit_bytes=60 * 2**20)
    middle, first, second, third, partial = pl.pallas_call(
        middle_kernel,
        out_shape=(
            jax.ShapeDtypeStruct((mid_rows, 128, tile_cols), BF16),
            jax.ShapeDtypeStruct(rows_of(6), F32),
            jax.ShapeDtypeStruct(rows_of(4), F32),
            jax.ShapeDtypeStruct(rows_of(4), F32),
            jax.ShapeDtypeStruct((ROWS, ROWS), F32),
        ),
        in_specs=[vmem, vmem],
        out_specs=(anywhere, anywhere, anywhere, anywhere, vmem),
        scratch_shapes=[
            *[pltpu.VMEM(rows_of(tile_rows), F32) for _ in range(3)],
            pltpu.VMEM((tile_rows, 5, 8, wide), F32),
            pltpu.VMEM((mid_rows, ROWS, tile_cols), BF16),
            pltpu.SemaphoreType.DMA((14 + mid_rows,)),
        ],
        compiler_params=params,
        cost_estimate=pl.CostEstimate(flops=10**9, bytes_accessed=20 * 10**6, transcendentals=0),
        name="middle",
    )(fields, side)
    edge, payload = pl.pallas_call(
        edge_kernel,
        out_shape=(
            jax.ShapeDtypeStruct((2 * HALO, 128, tile_cols), BF16),
            jax.ShapeDtypeStruct((32, 16, LANE), F32),
        ),
        in_specs=[vmem] * 9,
        out_specs=(anywhere, vmem),
        scratch_shapes=[
            *[pltpu.VMEM(rows_of(depth), F32) for _ in range(3)],
            pltpu.VMEM((depth, 5, 8, wide), F32),
            pltpu.VMEM((2 * HALO, ROWS, tile_cols), BF16),
            pltpu.VMEM((ROWS, ROWS), F32),
            pltpu.SemaphoreType.DMA((2 * HALO,)),
        ],
        compiler_params=params,
        name="edge",
    )(fields, side, low, high, first, second, third, partial, jnp.asarray(selection()))

    parts = lax.all_to_all(payload, ("y", "core", "x"), 0, 0, tiled=True)
    total = jnp.sum(parts, axis=0)
    parts = lax.all_to_all(
        jnp.broadcast_to(total[None], (lax.axis_size("z"), 16, LANE)), ("z",), 0, 0, tiled=True
    )

    out = pl.pallas_call(
        solve_kernel,
        out_shape=jax.ShapeDtypeStruct((CH * tile_rows, tile_cols), F32),
        in_specs=[pl.BlockSpec(memory_space=pltpu.SMEM), vmem, vmem, anywhere, anywhere],
        out_specs=anywhere,
        scratch_shapes=[
            pltpu.VMEM((mid_rows, 128, tile_cols), BF16),
            pltpu.VMEM((2 * HALO, 128, tile_cols), BF16),
            pltpu.VMEM((tile_cols // LANE, CH * tile_rows, LANE), F32),
            pltpu.SemaphoreType.DMA((2 + tile_cols // LANE,)),
        ],
        compiler_params=params,
        name="solve",
    )(shifts.T, parts, jnp.asarray(expansion()), middle, edge)
    return out.reshape(CH, tile_rows, tile_cols)


def solution(mesh):
    fine = Mesh(mesh.devices.reshape(16, 4, 2, 4), ("z", "y", "core", "x"))
    gx = ("z", "y", "core")
    in_specs = (P(None, gx, "x"), P(gx, "x"), P(None, gx, "x"), P())
    return jax.shard_map(
        per_device, mesh=fine, in_specs=in_specs, out_specs=P(None, gx, "x"), check_vma=False
    )
```

```python
import jax
import jax.numpy as jnp
import numpy as np
from jax import lax
from jax.experimental import pallas as pl
from jax.experimental.pallas import tpu as pltpu
from jax.sharding import Mesh
from jax.sharding import PartitionSpec as P

S = 4
THETA = (-8.0, -2.0, -14.0, -5.0)
SCALE = 8.0
CH = 12
HALO = 4
LANE = 128
HIGH = lax.Precision.HIGHEST
F32 = jnp.float32
BF16 = jnp.bfloat16
HI_AT = (0, 16, 32, 48, 128)
LO_AT = (64, 80, 96, 112, 144)
ROWS = 160


def selection():
    pick = np.zeros((128, ROWS), np.float32)
    for k in range(S + 1):
        for c in range(CH):
            i = k * CH + c
            at = i if i < 30 else i + 2
            pick[at, HI_AT[k] + c] = 1.0
            pick[at, LO_AT[k] + c] = 1.0
    return pick


def expansion():
    spread = np.zeros((64, 48), np.float32)
    for k in range(S):
        for c in range(CH):
            spread[k * 16 + c, k * CH + c] = 1.0
    return spread


def split(value):
    high = value.astype(BF16)
    return high, (value - high.astype(F32)).astype(BF16)


def coefficients(coef, at, field):
    shape = (8, field.shape[-1])
    spread = jnp.broadcast_to(field[1, 4:5, :], shape) * (1.0 / SCALE)
    drift_x = jnp.broadcast_to(field[1, 5:6, :], shape) * (0.5 / SCALE)
    drift_y = jnp.broadcast_to(field[1, 6:7, :], shape) * (0.5 / SCALE)
    coef[at, 0] = spread + drift_x
    coef[at, 1] = spread - drift_x
    coef[at, 2] = spread + drift_y
    coef[at, 3] = spread - drift_y
    coef[at, 4] = -4.0 * spread


def newton_row(coef, at, k, center, after, before):
    wide = center.shape[-1]
    return (
        coef[at, 0][None] * after
        + coef[at, 1][None] * before
        + coef[at, 2][None] * pltpu.roll(center, wide - 1, 2)
        + coef[at, 3][None] * pltpu.roll(center, 1, 2)
        + (coef[at, 4] - THETA[k] / SCALE)[None] * center
    )


def keep(pieces, at, k, value):
    cols = pieces.shape[-1]
    hi, lo = split(value[:, :, :cols].reshape(16, cols))
    pieces[at, HI_AT[k] : HI_AT[k] + 16, :] = hi
    pieces[at, LO_AT[k] : LO_AT[k] + 16, :] = lo


def add_gram(acc, rows):
    acc[...] += lax.dot_general(rows, rows, (((1,), (1,)), ((), ())), preferred_element_type=F32)


def middle_kernel(own, side, basis, first, second, third, acc, v1, v2, v3, coef, pieces, sems):
    tile_rows = own.shape[0]
    levels = (None, v1, v2, v3)
    acc[...] = jnp.zeros_like(acc)
    copies = []

    def start(source, target):
        copy = pltpu.make_async_copy(source, target, sems.at[len(copies)])
        copy.start()
        copies.append(copy)

    def get(k, r):
        if k:
            return levels[k][r]
        return jnp.concatenate([own[r], side[r]], axis=2)

    for front in range(1, tile_rows + 1):
        if front < tile_rows - 1:
            coefficients(coef, front, get(0, front))
        for k in range(S):
            r = front - k
            if k < r < tile_rows - 1 - k:
                value = newton_row(coef, r, k, get(k, r), get(k, r + 1), get(k, r - 1))
                if k < S - 1:
                    levels[k + 1][r] = value
                    group, at = (first, second, third)[k], export_at(k + 1, r, tile_rows)
                    if at is not None:
                        start(levels[k + 1].at[r], group.at[at])
                if HALO <= r < tile_rows - HALO:
                    keep(pieces, r - HALO, k + 1, value)
                    if k == 0:
                        keep(pieces, r - HALO, 0, get(0, r))
        r = front - S
        if HALO <= r < tile_rows - HALO:
            add_gram(acc, pieces[r - HALO])
            start(pieces.at[r - HALO, 0:128, :], basis.at[r - HALO])
    for copy in copies:
        copy.wait()


def export_at(k, r, tile_rows):
    low = {1: (1, 2, 3), 2: (2, 3), 3: (3, 4)}[k]
    rows = low + tuple(tile_rows - 1 - i for i in reversed(low))
    return rows.index(r) if r in rows else None


def edge_kernel(
    core, own, side, near, across, first, second, third, middle, pick, basis, payload, v1, v2, v3, coef, pieces, acc, sems
):
    tile_rows = own.shape[0]
    levels = (None, v1, v2, v3)
    exports = (None, first, second, third)
    acc[...] = middle[...]
    even = core[0] == 0
    copies = []

    def get(k, r):
        if k:
            at = export_at(k, r, tile_rows)
            return levels[k][r + HALO] if at is None else exports[k][at]
        if r < 0:
            return jnp.where(even, across[r + HALO], near[r + HALO])
        if r >= tile_rows:
            return jnp.where(even, near[r - tile_rows], across[r - tile_rows])
        return jnp.concatenate([own[r], side[r]], axis=2)

    def finish(at):
        add_gram(acc, pieces[at])
        copy = pltpu.make_async_copy(pieces.at[at, 0:128, :], basis.at[at], sems.at[at])
        copy.start()
        copies.append(copy)

    ready = []
    for far in (False, True):
        def place(i):
            return tile_rows - 1 - i if far else i

        def slot(i):
            return i + HALO if far else i

        for i in range(1 - HALO, HALO):
            coefficients(coef, place(i) + HALO, get(0, place(i)))
        for k in range(S):
            for i in range(k + 1 - HALO, k + 1):
                r = place(i)
                value = newton_row(coef, r + HALO, k, get(k, r), get(k, r + 1), get(k, r - 1))
                if k < S - 1:
                    levels[k + 1][r + HALO] = value
                if i >= 0:
                    keep(pieces, slot(i), k + 1, value)
                if k == S - 1:
                    ready.append(slot(i))
                if ready and (far or k == S - 1) and i % 2 == 1:
                    finish(ready.pop(0))
            for i in range(k + 1, HALO):
                if k < S - 1:
                    keep(pieces, slot(i), k + 1, get(k + 1, place(i)))
            if k == 0:
                for i in range(HALO):
                    keep(pieces, slot(i), 0, get(0, place(i)))
    for at in ready:
        finish(at)

    half = jnp.dot(pick[0:64, :], acc[...], precision=HIGH, preferred_element_type=F32)
    gram = lax.dot_general(half, pick[...], (((1,), (1,)), ((), ())), precision=HIGH, preferred_element_type=F32)
    row = lax.broadcasted_iota(jnp.int32, (32, 128), 0)
    column = lax.broadcasted_iota(jnp.int32, (32, 128), 1)
    one, two = gram[0:32], gram[32:64]
    cross = pltpu.roll(one, 96, 1)
    shifted = pltpu.roll(one, 32, 1)
    diagonal = jnp.sum(jnp.where(column == row + 32, two, 0.0), axis=1, keepdims=True)
    packed = jnp.where(row + 32 >= column, shifted, two)
    packed = jnp.where(column == 63, jnp.broadcast_to(diagonal, (32, 128)), packed)
    whole = jnp.where(column < 32, cross, packed)
    whole = jnp.where(column < 64, whole, 0.0)
    folded = whole[0:16] + pltpu.roll(whole[16:32], 64, 1)
    payload[...] = jnp.broadcast_to(folded[None], payload.shape)
    for copy in copies:
        copy.wait()


def gather_rows(right_side, diffusion, drift_field, strips, sems, at):
    tile_rows = diffusion.shape[0]
    first, second = CH * tile_rows, (CH + 1) * tile_rows
    cols = pl.ds(at[1] * LANE, LANE)
    copies = (
        (right_side.at[:, cols], strips.at[at[0], 0:first]),
        (diffusion.at[:, cols], strips.at[at[0], first:second]),
        (drift_field.at[:, cols], strips.at[at[0], second : second + 2 * tile_rows]),
    )
    copies = [pltpu.make_async_copy(a, b, sems.at[at[0], i]) for i, (a, b) in enumerate(copies)]
    for copy in copies:
        copy.start()
    return copies


def edges_kernel(right_side, diffusion, drift_field, left, right, strips, sems):
    tile_rows, tile_cols = diffusion.shape
    outs = (left, right)
    places = (0, tile_cols // LANE - 1)
    copies = [gather_rows(right_side, diffusion, drift_field, strips, sems, (i, p)) for i, p in enumerate(places)]
    for i in range(2):
        strips[i, 15 * tile_rows :] = jnp.zeros((tile_rows, LANE), F32)
        for copy in copies[i]:
            copy.wait()
        for r in range(tile_rows):
            for half in range(2):
                outs[i][r, half] = strips.at[i][pl.ds(8 * half * tile_rows + r, 8, stride=tile_rows), :]


def fields_kernel(right_side, diffusion, drift_field, fields, strips, sems):
    tile_rows, tile_cols = diffusion.shape
    count = tile_cols // LANE
    copies = [gather_rows(right_side, diffusion, drift_field, strips, sems, (i, i)) for i in range(count)]
    for i in range(count):
        strips[i, 15 * tile_rows :] = jnp.zeros((tile_rows, LANE), F32)
        for copy in copies[i]:
            copy.wait()
        for r in range(tile_rows):
            for half in range(2):
                fields[r, half, :, i * LANE : (i + 1) * LANE] = strips.at[i][
                    pl.ds(8 * half * tile_rows + r, 8, stride=tile_rows), :
                ]


def lane(shape):
    return lax.broadcasted_iota(jnp.int32, shape, len(shape) - 1)


def unpack(parts):
    total = parts[0]
    for i in range(1, parts.shape[0]):
        total = total + parts[i]
    row = lax.broadcasted_iota(jnp.int32, (32, 128), 0)
    column = lax.broadcasted_iota(jnp.int32, (32, 128), 1)
    whole = jnp.concatenate([total, pltpu.roll(total, 64, 1)], axis=0)
    whole = jnp.where(column < 64, whole, 0.0)
    flipped = jnp.concatenate([whole, jnp.zeros((96, 128), F32)], axis=0).T
    packed = pltpu.roll(whole, 96, 1)
    turned = flipped[32:64]
    diagonal = jnp.broadcast_to(whole[:, 63:64], (32, 128))
    first = jnp.where(row >= column, packed, turned)
    second = jnp.where(row < column, packed, turned)
    second = jnp.where(row == column, diagonal, second)
    left = column < 32
    top = jnp.where(left, first, pltpu.roll(whole, 32, 1))
    bottom = jnp.where(left, flipped[0:32], pltpu.roll(second, 32, 1))
    gram = jnp.concatenate([top, bottom], axis=0)
    gram = jnp.where(lane((64, 128)) < 30, gram, pltpu.roll(gram, 126, 1))
    return jnp.where(lax.broadcasted_iota(jnp.int32, (64, 128), 0) < 30, gram, pltpu.roll(gram, 62, 0))


def normal_systems(g, shifts):
    lanes = lane((48, 128))
    rows_id = lax.broadcasted_iota(jnp.int32, (48, 128), 0)
    theta_col = jnp.zeros((48, 128), F32)
    theta_row = jnp.zeros((48, 128), F32)
    for k in range(S):
        theta_row = jnp.where((rows_id >= 12 * k) & (rows_id < 12 * k + 12), THETA[k], theta_row)
        theta_col = jnp.where((lanes >= 12 * k) & (lanes < 12 * k + 12), THETA[k], theta_col)
    g0 = g[0:48]
    gd = pltpu.roll(g, 64 - 12, 0)[0:48]
    gr = pltpu.roll(g0, 128 - 12, 1)
    grd = pltpu.roll(gd, 128 - 12, 1)
    inside = lanes < 48
    at_rhs = lanes == 48
    systems = []
    for j in range(CH // 2):
        a = shifts[0, j]
        b = shifts[1, j]
        alpha_i = theta_row - a
        alpha_l = theta_col - a
        real = (alpha_i * alpha_l + b * b) * g0 + SCALE * (alpha_i * gr + alpha_l * gd) + SCALE * SCALE * grd
        imag = b * ((alpha_l - alpha_i) * g0 + SCALE * (gr - gd))
        g1 = pltpu.roll(g0, 48 - 2 * j, 1)
        g2 = pltpu.roll(g0, 47 - 2 * j, 1)
        gd1 = pltpu.roll(gd, 48 - 2 * j, 1)
        gd2 = pltpu.roll(gd, 47 - 2 * j, 1)
        rhs_real = alpha_i * g1 - b * g2 + SCALE * gd1
        rhs_imag = alpha_i * g2 + b * g1 + SCALE * gd2
        real = jnp.where(inside, real, jnp.where(at_rhs, rhs_real, 0.0))
        imag = jnp.where(inside, imag, jnp.where(at_rhs, rhs_imag, 0.0))
        system = real + pltpu.roll(imag, 64, 1)
        systems.append([system[8 * i : 8 * i + 8] for i in range(6)])
    return systems


def column_of(block, at):
    return jnp.broadcast_to(block[:, at : at + 1], (8, 128))


def eliminate(systems):
    flip = jnp.where(lane((1, 128)) < 64, -1.0, 1.0)
    rows_id = lax.broadcasted_iota(jnp.int32, (8, 128), 0)
    for k in range(0, 48, 2):
        at, p = k // 8, k % 8
        for blocks in systems:
            pivot = blocks[at]
            row0, row1 = pivot[p : p + 1], pivot[p + 1 : p + 2]
            turn0 = pltpu.roll(row0, 64, 1) * flip
            turn1 = pltpu.roll(row1, 64, 1) * flip
            columns = [
                [column_of(b, c) for c in (k, 64 + k, k + 1, 65 + k)] for b in blocks
            ]
            c0r, _, c1r, c1i = columns[at]
            a, zr, zi, d = c0r[p : p + 1], c1r[p : p + 1], c1i[p : p + 1], c1r[p + 1 : p + 2]
            scale = 1.0 / (a * d - (zr * zr + zi * zi))
            a, zr, zi, d = a * scale, zr * scale, zi * scale, d * scale
            x0 = d * row0 - (zr * row1 + zi * turn1)
            x1 = a * row1 - (zr * row0 - zi * turn0)
            t0 = d * turn0 - (zr * turn1 - zi * row1)
            t1 = a * turn1 - (zr * turn0 + zi * row0)
            for i in range(6):
                c0r, c0i, c1r, c1i = columns[i]
                update = blocks[i] - ((c0r * x0 + c0i * t0) + (c1r * x1 + c1i * t1))
                if i == at:
                    update = jnp.where(rows_id == p, x0, jnp.where(rows_id == p + 1, x1, update))
                blocks[i] = update
    return systems


def solve_kernel(shifts, parts, spread, middle_hbm, edge_hbm, out, middle, edge, mixed, sems):
    tile_rows = middle.shape[0] + edge.shape[0]
    strips = mixed.shape[0]
    copies = [
        pltpu.make_async_copy(middle_hbm, middle, sems.at[0]),
        pltpu.make_async_copy(edge_hbm, edge, sems.at[1]),
    ]
    for copy in copies:
        copy.start()

    systems = eliminate(normal_systems(unpack(parts), shifts))
    lanes = lane((48, 128))
    mix = jnp.zeros((48, 128), F32)
    for j, blocks in enumerate(systems):
        m = jnp.concatenate(blocks, axis=0)
        mix = jnp.where(lanes == 2 * j, jnp.broadcast_to(m[:, 48:49], (48, 128)), mix)
        mix = jnp.where(lanes == 2 * j + 1, jnp.broadcast_to(m[:, 112:113], (48, 128)), mix)
    mix = jnp.dot(spread[...], mix, precision=HIGH, preferred_element_type=F32)
    mix_hi, mix_lo = split(mix)
    weights = mix_hi.astype(F32) + pltpu.roll(mix_lo.astype(F32), 16, 1)
    weights = jnp.concatenate([weights, weights], axis=0).T[0:32].astype(BF16)

    for copy in copies:
        copy.wait()

    def combine(pieces, r):
        both = jnp.dot(weights, pieces, preferred_element_type=F32)
        both = both[0:16] + both[16:32]
        for j in range(strips):
            mixed.at[j][pl.ds(r, CH, stride=tile_rows), :] = both[0:CH, j * LANE : (j + 1) * LANE]

    for i in range(tile_rows - 2 * HALO):
        combine(middle[i], i + HALO)
    for i in range(HALO):
        combine(edge[i], i)
        combine(edge[i + HALO], tile_rows - 1 - i)
    copies = [
        pltpu.make_async_copy(mixed.at[j], out.at[:, j * LANE : (j + 1) * LANE], sems.at[2 + j]) for j in range(strips)
    ]
    for copy in copies:
        copy.start()
    for copy in copies:
        copy.wait()


def per_device(right_side, diffusion, drift_field, shifts):
    tile_rows, tile_cols = right_side.shape[1:]
    wide, mid_rows, depth = tile_cols + LANE, tile_rows - 2 * HALO, tile_rows + 2 * HALO
    anywhere = pl.BlockSpec(memory_space=pl.ANY)
    vmem = pl.BlockSpec(memory_space=pltpu.VMEM)
    far = pl.BlockSpec(memory_space=pltpu.HBM)
    scalar = pl.BlockSpec(memory_space=pltpu.SMEM)

    def params(mib):
        return pltpu.CompilerParams(vmem_limit_bytes=mib * 2**20)

    count = tile_cols // LANE

    def rows_of(n, width=wide):
        return (n, 2, 8, width)

    raw = (
        right_side.reshape(CH * tile_rows, tile_cols),
        diffusion,
        drift_field.reshape(2 * tile_rows, tile_cols),
    )
    left, right = pl.pallas_call(
        edges_kernel,
        out_shape=[jax.ShapeDtypeStruct(rows_of(tile_rows, LANE), F32)] * 2,
        in_specs=[anywhere] * 3,
        scratch_shapes=[pltpu.VMEM((2, 16 * tile_rows, LANE), F32), pltpu.SemaphoreType.DMA((2, 3))],
        compiler_params=params(60),
        name="edges",
    )(*raw)
    gy = lax.axis_size("x")
    from_left = lax.ppermute(right, "x", [(i, i + 1) for i in range(gy - 1)])
    from_right = lax.ppermute(left, "x", [(i + 1, i) for i in range(gy - 1)])
    side = jnp.where(lax.broadcasted_iota(jnp.int32, from_left.shape, 3) < LANE // 2, from_right, from_left)
    fields = pl.pallas_call(
        fields_kernel,
        out_shape=jax.ShapeDtypeStruct(rows_of(tile_rows, tile_cols), F32),
        in_specs=[anywhere] * 3,
        scratch_shapes=[pltpu.VMEM((count, 16 * tile_rows, LANE), F32), pltpu.SemaphoreType.DMA((count, 3))],
        compiler_params=params(60),
        cost_estimate=pl.CostEstimate(flops=10**6, bytes_accessed=4 * 10**6, transcendentals=0),
        name="fields",
    )(*raw)
    core = lax.axis_index("core")
    start = jnp.concatenate([fields[:HALO], side[:HALO]], axis=3)
    end = jnp.concatenate([fields[-HALO:], side[-HALO:]], axis=3)
    gx = ("z", "y", "core")
    ring = lax.axis_size(gx)
    across = lax.ppermute(
        jnp.where(core == 0, start, end), gx, [(i, (i + 2 * (i % 2) - 1) % ring) for i in range(ring)]
    )
    near = lax.ppermute(jnp.where(core == 0, end, start), "core", [(0, 1), (1, 0)])
    middle, first, second, third, partial = pl.pallas_call(
        middle_kernel,
        out_shape=(
            jax.ShapeDtypeStruct((mid_rows, 128, tile_cols), BF16),
            jax.ShapeDtypeStruct(rows_of(6), F32),
            jax.ShapeDtypeStruct(rows_of(4), F32),
            jax.ShapeDtypeStruct(rows_of(4), F32),
            jax.ShapeDtypeStruct((ROWS, ROWS), F32),
        ),
        in_specs=[vmem, vmem],
        out_specs=(far, anywhere, anywhere, anywhere, vmem),
        scratch_shapes=[
            *[pltpu.VMEM(rows_of(tile_rows), F32) for _ in range(3)],
            pltpu.VMEM((tile_rows, 5, 8, wide), F32),
            pltpu.VMEM((mid_rows, ROWS, tile_cols), BF16),
            pltpu.SemaphoreType.DMA((14 + mid_rows,)),
        ],
        compiler_params=params(28),
        cost_estimate=pl.CostEstimate(flops=10**9, bytes_accessed=20 * 10**6, transcendentals=0),
        name="middle",
    )(fields, side)
    edge, payload = pl.pallas_call(
        edge_kernel,
        out_shape=(
            jax.ShapeDtypeStruct((2 * HALO, 128, tile_cols), BF16),
            jax.ShapeDtypeStruct((32, 16, LANE), F32),
        ),
        in_specs=[scalar, *[vmem] * 9],
        out_specs=(far, vmem),
        scratch_shapes=[
            *[pltpu.VMEM(rows_of(depth), F32) for _ in range(3)],
            pltpu.VMEM((depth, 5, 8, wide), F32),
            pltpu.VMEM((2 * HALO, ROWS, tile_cols), BF16),
            pltpu.VMEM((ROWS, ROWS), F32),
            pltpu.SemaphoreType.DMA((2 * HALO,)),
        ],
        compiler_params=params(40),
        name="edge",
    )(core.reshape(1), fields, side, near, across, first, second, third, partial, jnp.asarray(selection()))

    parts = lax.all_to_all(payload, ("y", "core", "x"), 0, 0, tiled=True)
    total = jnp.sum(parts, axis=0)
    parts = lax.all_to_all(
        jnp.broadcast_to(total[None], (lax.axis_size("z"), 16, LANE)), ("z",), 0, 0, tiled=True
    )

    out = pl.pallas_call(
        solve_kernel,
        out_shape=jax.ShapeDtypeStruct((CH * tile_rows, tile_cols), F32),
        in_specs=[scalar, vmem, vmem, far, far],
        out_specs=anywhere,
        scratch_shapes=[
            pltpu.VMEM((mid_rows, 128, tile_cols), BF16),
            pltpu.VMEM((2 * HALO, 128, tile_cols), BF16),
            pltpu.VMEM((tile_cols // LANE, CH * tile_rows, LANE), F32),
            pltpu.SemaphoreType.DMA((2 + tile_cols // LANE,)),
        ],
        compiler_params=params(60),
        name="solve",
    )(shifts.T, parts, jnp.asarray(expansion()), middle, edge)
    return out.reshape(CH, tile_rows, tile_cols)


def solution(mesh):
    fine = Mesh(mesh.devices.reshape(16, 4, 2, 4), ("z", "y", "core", "x"))
    gx = ("z", "y", "core")
    in_specs = (P(None, gx, "x"), P(gx, "x"), P(None, gx, "x"), P())
    return jax.shard_map(
        per_device, mesh=fine, in_specs=in_specs, out_specs=P(None, gx, "x"), check_vma=False
    )
```

```python
import jax
import jax.numpy as jnp
import numpy as np
from jax import lax
from jax.experimental import pallas as pl
from jax.experimental.pallas import tpu as pltpu
from jax.sharding import Mesh
from jax.sharding import PartitionSpec as P

S = 4
THETA = (-8.0, -2.0, -14.0, -5.0)
SCALE = 8.0
CH = 12
HALO = 4
LANE = 128
HIGH = lax.Precision.HIGHEST
F32 = jnp.float32
BF16 = jnp.bfloat16
HI_AT = (0, 16, 32, 48, 128)
LO_AT = (64, 80, 96, 112, 144)
ROWS = 160


def selection():
    pick = np.zeros((128, ROWS), np.float32)
    for k in range(S + 1):
        for c in range(CH):
            i = k * CH + c
            at = i if i < 30 else i + 2
            pick[at, HI_AT[k] + c] = 1.0
            pick[at, LO_AT[k] + c] = 1.0
    return pick


def expansion():
    spread = np.zeros((64, 48), np.float32)
    for k in range(S):
        for c in range(CH):
            spread[k * 16 + c, k * CH + c] = 1.0
    return spread


def split(value):
    high = value.astype(BF16)
    return high, (value - high.astype(F32)).astype(BF16)


def coefficients(coef, at, field):
    shape = (8, field.shape[-1])
    spread = jnp.broadcast_to(field[1, 4:5, :], shape) * (1.0 / SCALE)
    drift_x = jnp.broadcast_to(field[1, 5:6, :], shape) * (0.5 / SCALE)
    drift_y = jnp.broadcast_to(field[1, 6:7, :], shape) * (0.5 / SCALE)
    coef[at, 0] = spread + drift_x
    coef[at, 1] = spread - drift_x
    coef[at, 2] = spread + drift_y
    coef[at, 3] = spread - drift_y
    coef[at, 4] = -4.0 * spread


def newton_row(coef, at, k, center, after, before):
    wide = center.shape[-1]
    return (
        coef[at, 0][None] * after
        + coef[at, 1][None] * before
        + coef[at, 2][None] * pltpu.roll(center, wide - 1, 2)
        + coef[at, 3][None] * pltpu.roll(center, 1, 2)
        + (coef[at, 4] - THETA[k] / SCALE)[None] * center
    )


def keep(pieces, at, k, value):
    cols = pieces.shape[-1]
    hi, lo = split(value[:, :, :cols].reshape(16, cols))
    pieces[at, HI_AT[k] : HI_AT[k] + 16, :] = hi
    pieces[at, LO_AT[k] : LO_AT[k] + 16, :] = lo


def add_gram(acc, rows):
    acc[...] += lax.dot_general(rows, rows, (((1,), (1,)), ((), ())), preferred_element_type=F32)


def middle_kernel(own, side, basis, first, second, third, acc, v1, v2, v3, coef, pieces, sems):
    tile_rows = own.shape[0]
    levels = (None, v1, v2, v3)
    acc[...] = jnp.zeros_like(acc)
    copies = []

    def start(source, target):
        copy = pltpu.make_async_copy(source, target, sems.at[len(copies)])
        copy.start()
        copies.append(copy)

    def get(k, r):
        if k:
            return levels[k][r]
        return jnp.concatenate([own[r], side[r]], axis=2)

    for front in range(1, tile_rows + 1):
        if front < tile_rows - 1:
            coefficients(coef, front, get(0, front))
        for k in range(S):
            r = front - k
            if k < r < tile_rows - 1 - k:
                value = newton_row(coef, r, k, get(k, r), get(k, r + 1), get(k, r - 1))
                if k < S - 1:
                    levels[k + 1][r] = value
                    group, at = (first, second, third)[k], export_at(k + 1, r, tile_rows)
                    if at is not None:
                        start(levels[k + 1].at[r], group.at[at])
                if HALO <= r < tile_rows - HALO:
                    keep(pieces, r - HALO, k + 1, value)
                    if k == 0:
                        keep(pieces, r - HALO, 0, get(0, r))
        r = front - S
        if HALO <= r < tile_rows - HALO:
            add_gram(acc, pieces[r - HALO])
            start(pieces.at[r - HALO, 0:128, :], basis.at[r - HALO])
    for copy in copies:
        copy.wait()


def export_at(k, r, tile_rows):
    low = {1: (1, 2, 3), 2: (2, 3), 3: (3, 4)}[k]
    rows = low + tuple(tile_rows - 1 - i for i in reversed(low))
    return rows.index(r) if r in rows else None


def edge_kernel(
    core, own, side, near, across, first, second, third, middle, pick, basis, payload, v1, v2, v3, coef, pieces, acc, sems
):
    tile_rows = own.shape[0]
    levels = (None, v1, v2, v3)
    exports = (None, first, second, third)
    acc[...] = middle[...]
    even = core[0] == 0
    copies = []

    def get(k, r):
        if k:
            at = export_at(k, r, tile_rows)
            return levels[k][r + HALO] if at is None else exports[k][at]
        if r < 0:
            return jnp.where(even, across[r + HALO], near[r + HALO])
        if r >= tile_rows:
            return jnp.where(even, near[r - tile_rows], across[r - tile_rows])
        return jnp.concatenate([own[r], side[r]], axis=2)

    def finish(at):
        add_gram(acc, pieces[at])
        copy = pltpu.make_async_copy(pieces.at[at, 0:128, :], basis.at[at], sems.at[at])
        copy.start()
        copies.append(copy)

    ready = []
    for far in (False, True):
        def place(i):
            return tile_rows - 1 - i if far else i

        def slot(i):
            return i + HALO if far else i

        for i in range(1 - HALO, HALO):
            coefficients(coef, place(i) + HALO, get(0, place(i)))
        for k in range(S):
            for i in range(k + 1 - HALO, k + 1):
                r = place(i)
                value = newton_row(coef, r + HALO, k, get(k, r), get(k, r + 1), get(k, r - 1))
                if k < S - 1:
                    levels[k + 1][r + HALO] = value
                if i >= 0:
                    keep(pieces, slot(i), k + 1, value)
                if k == S - 1:
                    ready.append(slot(i))
                if ready and (far or k == S - 1) and i % 2 == 1:
                    finish(ready.pop(0))
            for i in range(k + 1, HALO):
                if k < S - 1:
                    keep(pieces, slot(i), k + 1, get(k + 1, place(i)))
            if k == 0:
                for i in range(HALO):
                    keep(pieces, slot(i), 0, get(0, place(i)))
    for at in ready:
        finish(at)

    half = jnp.dot(pick[0:64, :], acc[...], precision=HIGH, preferred_element_type=F32)
    gram = lax.dot_general(half, pick[...], (((1,), (1,)), ((), ())), precision=HIGH, preferred_element_type=F32)
    row = lax.broadcasted_iota(jnp.int32, (32, 128), 0)
    column = lax.broadcasted_iota(jnp.int32, (32, 128), 1)
    one, two = gram[0:32], gram[32:64]
    cross = pltpu.roll(one, 96, 1)
    shifted = pltpu.roll(one, 32, 1)
    diagonal = jnp.sum(jnp.where(column == row + 32, two, 0.0), axis=1, keepdims=True)
    packed = jnp.where(row + 32 >= column, shifted, two)
    packed = jnp.where(column == 63, jnp.broadcast_to(diagonal, (32, 128)), packed)
    whole = jnp.where(column < 32, cross, packed)
    whole = jnp.where(column < 64, whole, 0.0)
    folded = whole[0:16] + pltpu.roll(whole[16:32], 64, 1)
    payload[...] = jnp.broadcast_to(folded[None], payload.shape)
    for copy in copies:
        copy.wait()


def gather_rows(right_side, diffusion, drift_field, strips, sems, at):
    tile_rows = diffusion.shape[0]
    first, second = CH * tile_rows, (CH + 1) * tile_rows
    cols = pl.ds(at[1] * LANE, LANE)
    copies = (
        (right_side.at[:, cols], strips.at[at[0], 0:first]),
        (diffusion.at[:, cols], strips.at[at[0], first:second]),
        (drift_field.at[:, cols], strips.at[at[0], second : second + 2 * tile_rows]),
    )
    copies = [pltpu.make_async_copy(a, b, sems.at[at[0], i]) for i, (a, b) in enumerate(copies)]
    for copy in copies:
        copy.start()
    return copies


def edges_kernel(right_side, diffusion, drift_field, left, right, strips, sems):
    tile_rows, tile_cols = diffusion.shape
    outs = (left, right)
    places = (0, tile_cols // LANE - 1)
    copies = [gather_rows(right_side, diffusion, drift_field, strips, sems, (i, p)) for i, p in enumerate(places)]
    for i in range(2):
        strips[i, 15 * tile_rows :] = jnp.zeros((tile_rows, LANE), F32)
        for copy in copies[i]:
            copy.wait()
        for r in range(tile_rows):
            for half in range(2):
                outs[i][r, half] = strips.at[i][pl.ds(8 * half * tile_rows + r, 8, stride=tile_rows), :]


def fields_kernel(right_side, diffusion, drift_field, fields, strips, sems):
    tile_rows, tile_cols = diffusion.shape
    count = tile_cols // LANE
    copies = [gather_rows(right_side, diffusion, drift_field, strips, sems, (i, i)) for i in range(count)]
    for i in range(count):
        strips[i, 15 * tile_rows :] = jnp.zeros((tile_rows, LANE), F32)
        for copy in copies[i]:
            copy.wait()
        for r in range(tile_rows):
            for half in range(2):
                fields[r, half, :, i * LANE : (i + 1) * LANE] = strips.at[i][
                    pl.ds(8 * half * tile_rows + r, 8, stride=tile_rows), :
                ]


def lane(shape):
    return lax.broadcasted_iota(jnp.int32, shape, len(shape) - 1)


def unpack(parts):
    total = parts[0]
    for i in range(1, parts.shape[0]):
        total = total + parts[i]
    row = lax.broadcasted_iota(jnp.int32, (32, 128), 0)
    column = lax.broadcasted_iota(jnp.int32, (32, 128), 1)
    whole = jnp.concatenate([total, pltpu.roll(total, 64, 1)], axis=0)
    whole = jnp.where(column < 64, whole, 0.0)
    flipped = jnp.concatenate([whole, jnp.zeros((96, 128), F32)], axis=0).T
    packed = pltpu.roll(whole, 96, 1)
    turned = flipped[32:64]
    diagonal = jnp.broadcast_to(whole[:, 63:64], (32, 128))
    first = jnp.where(row >= column, packed, turned)
    second = jnp.where(row < column, packed, turned)
    second = jnp.where(row == column, diagonal, second)
    left = column < 32
    top = jnp.where(left, first, pltpu.roll(whole, 32, 1))
    bottom = jnp.where(left, flipped[0:32], pltpu.roll(second, 32, 1))
    gram = jnp.concatenate([top, bottom], axis=0)
    gram = jnp.where(lane((64, 128)) < 30, gram, pltpu.roll(gram, 126, 1))
    return jnp.where(lax.broadcasted_iota(jnp.int32, (64, 128), 0) < 30, gram, pltpu.roll(gram, 62, 0))


def normal_systems(g, shifts):
    lanes = lane((48, 128))
    rows_id = lax.broadcasted_iota(jnp.int32, (48, 128), 0)
    theta_col = jnp.zeros((48, 128), F32)
    theta_row = jnp.zeros((48, 128), F32)
    for k in range(S):
        theta_row = jnp.where((rows_id >= 12 * k) & (rows_id < 12 * k + 12), THETA[k], theta_row)
        theta_col = jnp.where((lanes >= 12 * k) & (lanes < 12 * k + 12), THETA[k], theta_col)
    g0 = g[0:48]
    gd = pltpu.roll(g, 64 - 12, 0)[0:48]
    gr = pltpu.roll(g0, 128 - 12, 1)
    grd = pltpu.roll(gd, 128 - 12, 1)
    inside = lanes < 48
    at_rhs = lanes == 48
    systems = []
    for j in range(CH // 2):
        a = shifts[0, j]
        b = shifts[1, j]
        alpha_i = theta_row - a
        alpha_l = theta_col - a
        real = (alpha_i * alpha_l + b * b) * g0 + SCALE * (alpha_i * gr + alpha_l * gd) + SCALE * SCALE * grd
        imag = b * ((alpha_l - alpha_i) * g0 + SCALE * (gr - gd))
        g1 = pltpu.roll(g0, 48 - 2 * j, 1)
        g2 = pltpu.roll(g0, 47 - 2 * j, 1)
        gd1 = pltpu.roll(gd, 48 - 2 * j, 1)
        gd2 = pltpu.roll(gd, 47 - 2 * j, 1)
        rhs_real = alpha_i * g1 - b * g2 + SCALE * gd1
        rhs_imag = alpha_i * g2 + b * g1 + SCALE * gd2
        real = jnp.where(inside, real, jnp.where(at_rhs, rhs_real, 0.0))
        imag = jnp.where(inside, imag, jnp.where(at_rhs, rhs_imag, 0.0))
        system = real + pltpu.roll(imag, 64, 1)
        systems.append([system[8 * i : 8 * i + 8] for i in range(6)])
    return systems


def column_of(block, at):
    return jnp.broadcast_to(block[:, at : at + 1], (8, 128))


def eliminate(systems):
    flip = jnp.where(lane((1, 128)) < 64, -1.0, 1.0)
    rows_id = lax.broadcasted_iota(jnp.int32, (8, 128), 0)
    for k in range(0, 48, 2):
        at, p = k // 8, k % 8
        for blocks in systems:
            pivot = blocks[at]
            row0, row1 = pivot[p : p + 1], pivot[p + 1 : p + 2]
            turn0 = pltpu.roll(row0, 64, 1) * flip
            turn1 = pltpu.roll(row1, 64, 1) * flip
            columns = [
                [column_of(b, c) for c in (k, 64 + k, k + 1, 65 + k)] for b in blocks
            ]
            c0r, _, c1r, c1i = columns[at]
            a, zr, zi, d = c0r[p : p + 1], c1r[p : p + 1], c1i[p : p + 1], c1r[p + 1 : p + 2]
            scale = 1.0 / (a * d - (zr * zr + zi * zi))
            a, zr, zi, d = a * scale, zr * scale, zi * scale, d * scale
            x0 = d * row0 - (zr * row1 + zi * turn1)
            x1 = a * row1 - (zr * row0 - zi * turn0)
            t0 = d * turn0 - (zr * turn1 - zi * row1)
            t1 = a * turn1 - (zr * turn0 + zi * row0)
            for i in range(6):
                c0r, c0i, c1r, c1i = columns[i]
                update = blocks[i] - ((c0r * x0 + c0i * t0) + (c1r * x1 + c1i * t1))
                if i == at:
                    update = jnp.where(rows_id == p, x0, jnp.where(rows_id == p + 1, x1, update))
                blocks[i] = update
    return systems


def solve_kernel(shifts, parts, spread, middle_hbm, edge_hbm, out, middle, edge, mixed, sems):
    tile_rows = middle.shape[0] + edge.shape[0]
    strips = mixed.shape[0]
    copies = [
        pltpu.make_async_copy(middle_hbm, middle, sems.at[0]),
        pltpu.make_async_copy(edge_hbm, edge, sems.at[1]),
    ]
    for copy in copies:
        copy.start()

    systems = eliminate(normal_systems(unpack(parts), shifts))
    lanes = lane((48, 128))
    mix = jnp.zeros((48, 128), F32)
    for j, blocks in enumerate(systems):
        m = jnp.concatenate(blocks, axis=0)
        mix = jnp.where(lanes == 2 * j, jnp.broadcast_to(m[:, 48:49], (48, 128)), mix)
        mix = jnp.where(lanes == 2 * j + 1, jnp.broadcast_to(m[:, 112:113], (48, 128)), mix)
    mix = jnp.dot(spread[...], mix, precision=HIGH, preferred_element_type=F32)
    mix_hi, mix_lo = split(mix)
    weights = mix_hi.astype(F32) + pltpu.roll(mix_lo.astype(F32), 16, 1)
    weights = jnp.concatenate([weights, weights], axis=0).T[0:32].astype(BF16)

    for copy in copies:
        copy.wait()

    def combine(pieces, r):
        both = jnp.dot(weights, pieces, preferred_element_type=F32)
        both = both[0:16] + both[16:32]
        for j in range(strips):
            mixed.at[j][pl.ds(r, CH, stride=tile_rows), :] = both[0:CH, j * LANE : (j + 1) * LANE]

    for i in range(tile_rows - 2 * HALO):
        combine(middle[i], i + HALO)
    for i in range(HALO):
        combine(edge[i], i)
        combine(edge[i + HALO], tile_rows - 1 - i)
    copies = [
        pltpu.make_async_copy(mixed.at[j], out.at[:, j * LANE : (j + 1) * LANE], sems.at[2 + j]) for j in range(strips)
    ]
    for copy in copies:
        copy.start()
    for copy in copies:
        copy.wait()


def per_device(right_side, diffusion, drift_field, shifts):
    tile_rows, tile_cols = right_side.shape[1:]
    wide, mid_rows, depth = tile_cols + LANE, tile_rows - 2 * HALO, tile_rows + 2 * HALO
    anywhere = pl.BlockSpec(memory_space=pl.ANY)
    vmem = pl.BlockSpec(memory_space=pltpu.VMEM)
    far = pl.BlockSpec(memory_space=pltpu.HBM)
    scalar = pl.BlockSpec(memory_space=pltpu.SMEM)

    def params(mib):
        return pltpu.CompilerParams(vmem_limit_bytes=mib * 2**20)

    count = tile_cols // LANE

    def rows_of(n, width=wide):
        return (n, 2, 8, width)

    raw = (
        right_side.reshape(CH * tile_rows, tile_cols),
        diffusion,
        drift_field.reshape(2 * tile_rows, tile_cols),
    )
    left, right = pl.pallas_call(
        edges_kernel,
        out_shape=[jax.ShapeDtypeStruct(rows_of(tile_rows, LANE), F32)] * 2,
        in_specs=[anywhere] * 3,
        scratch_shapes=[pltpu.VMEM((2, 16 * tile_rows, LANE), F32), pltpu.SemaphoreType.DMA((2, 3))],
        compiler_params=params(60),
        name="edges",
    )(*raw)
    gy = lax.axis_size("x")
    from_left = lax.ppermute(right, "x", [(i, i + 1) for i in range(gy - 1)])
    from_right = lax.ppermute(left, "x", [(i + 1, i) for i in range(gy - 1)])
    side = jnp.where(lax.broadcasted_iota(jnp.int32, from_left.shape, 3) < LANE // 2, from_right, from_left)
    fields = pl.pallas_call(
        fields_kernel,
        out_shape=jax.ShapeDtypeStruct(rows_of(tile_rows, tile_cols), F32),
        in_specs=[anywhere] * 3,
        scratch_shapes=[pltpu.VMEM((count, 16 * tile_rows, LANE), F32), pltpu.SemaphoreType.DMA((count, 3))],
        compiler_params=params(60),
        cost_estimate=pl.CostEstimate(flops=10**6, bytes_accessed=4 * 10**6, transcendentals=0),
        name="fields",
    )(*raw)
    core = lax.axis_index("core")
    start = jnp.concatenate([fields[:HALO], side[:HALO]], axis=3)
    end = jnp.concatenate([fields[-HALO:], side[-HALO:]], axis=3)
    gx = ("z", "y", "core")
    ring = lax.axis_size(gx)
    across = lax.ppermute(
        jnp.where(core == 0, start, end), gx, [(i, (i + 2 * (i % 2) - 1) % ring) for i in range(ring)]
    )
    near = lax.ppermute(jnp.where(core == 0, end, start), "core", [(0, 1), (1, 0)])
    middle, first, second, third, partial = pl.pallas_call(
        middle_kernel,
        out_shape=(
            jax.ShapeDtypeStruct((mid_rows, 128, tile_cols), BF16),
            jax.ShapeDtypeStruct(rows_of(6), F32),
            jax.ShapeDtypeStruct(rows_of(4), F32),
            jax.ShapeDtypeStruct(rows_of(4), F32),
            jax.ShapeDtypeStruct((ROWS, ROWS), F32),
        ),
        in_specs=[vmem, vmem],
        out_specs=(far, anywhere, anywhere, anywhere, vmem),
        scratch_shapes=[
            *[pltpu.VMEM(rows_of(tile_rows), F32) for _ in range(3)],
            pltpu.VMEM((tile_rows, 5, 8, wide), F32),
            pltpu.VMEM((mid_rows, ROWS, tile_cols), BF16),
            pltpu.SemaphoreType.DMA((14 + mid_rows,)),
        ],
        compiler_params=params(60),
        cost_estimate=pl.CostEstimate(flops=10**9, bytes_accessed=20 * 10**6, transcendentals=0),
        name="middle",
    )(fields, side)
    edge, payload = pl.pallas_call(
        edge_kernel,
        out_shape=(
            jax.ShapeDtypeStruct((2 * HALO, 128, tile_cols), BF16),
            jax.ShapeDtypeStruct((32, 16, LANE), F32),
        ),
        in_specs=[scalar, *[vmem] * 9],
        out_specs=(far, vmem),
        scratch_shapes=[
            *[pltpu.VMEM(rows_of(depth), F32) for _ in range(3)],
            pltpu.VMEM((depth, 5, 8, wide), F32),
            pltpu.VMEM((2 * HALO, ROWS, tile_cols), BF16),
            pltpu.VMEM((ROWS, ROWS), F32),
            pltpu.SemaphoreType.DMA((2 * HALO,)),
        ],
        compiler_params=params(60),
        name="edge",
    )(core.reshape(1), fields, side, near, across, first, second, third, partial, jnp.asarray(selection()))

    parts = lax.all_to_all(payload, ("y", "core", "x"), 0, 0, tiled=True)
    total = jnp.sum(parts, axis=0)
    parts = lax.all_to_all(
        jnp.broadcast_to(total[None], (lax.axis_size("z"), 16, LANE)), ("z",), 0, 0, tiled=True
    )

    out = pl.pallas_call(
        solve_kernel,
        out_shape=jax.ShapeDtypeStruct((CH * tile_rows, tile_cols), F32),
        in_specs=[scalar, vmem, vmem, far, far],
        out_specs=anywhere,
        scratch_shapes=[
            pltpu.VMEM((mid_rows, 128, tile_cols), BF16),
            pltpu.VMEM((2 * HALO, 128, tile_cols), BF16),
            pltpu.VMEM((tile_cols // LANE, CH * tile_rows, LANE), F32),
            pltpu.SemaphoreType.DMA((2 + tile_cols // LANE,)),
        ],
        compiler_params=params(60),
        name="solve",
    )(shifts.T, parts, jnp.asarray(expansion()), middle, edge)
    return out.reshape(CH, tile_rows, tile_cols)


def solution(mesh):
    fine = Mesh(mesh.devices.reshape(16, 4, 2, 4), ("z", "y", "core", "x"))
    gx = ("z", "y", "core")
    in_specs = (P(None, gx, "x"), P(gx, "x"), P(None, gx, "x"), P())
    return jax.shard_map(
        per_device, mesh=fine, in_specs=in_specs, out_specs=P(None, gx, "x"), check_vma=False
    )
```

```python
import jax
import jax.numpy as jnp
import numpy as np
from jax import lax
from jax.experimental import pallas as pl
from jax.experimental.pallas import tpu as pltpu
from jax.sharding import Mesh
from jax.sharding import PartitionSpec as P

S = 4
THETA = (-8.0, -2.0, -14.0, -5.0)
SCALE = 8.0
CH = 12
HALO = 4
LANE = 128
HIGH = lax.Precision.HIGHEST
F32 = jnp.float32
BF16 = jnp.bfloat16
HI_AT = (0, 16, 32, 48, 128)
LO_AT = (64, 80, 96, 112, 144)
ROWS = 160


def selection():
    pick = np.zeros((128, ROWS), np.float32)
    for k in range(S + 1):
        for c in range(CH):
            i = k * CH + c
            at = i if i < 30 else i + 2
            pick[at, HI_AT[k] + c] = 1.0
            pick[at, LO_AT[k] + c] = 1.0
    return pick


def expansion():
    spread = np.zeros((64, 48), np.float32)
    for k in range(S):
        for c in range(CH):
            spread[k * 16 + c, k * CH + c] = 1.0
    return spread


def split(value):
    high = value.astype(BF16)
    return high, (value - high.astype(F32)).astype(BF16)


def coefficients(coef, at, field):
    shape = (8, field.shape[-1])
    spread = jnp.broadcast_to(field[1, 4:5, :], shape) * (1.0 / SCALE)
    drift_x = jnp.broadcast_to(field[1, 5:6, :], shape) * (0.5 / SCALE)
    drift_y = jnp.broadcast_to(field[1, 6:7, :], shape) * (0.5 / SCALE)
    coef[at, 0] = spread + drift_x
    coef[at, 1] = spread - drift_x
    coef[at, 2] = spread + drift_y
    coef[at, 3] = spread - drift_y
    coef[at, 4] = -4.0 * spread


def newton_row(coef, at, k, center, after, before):
    wide = center.shape[-1]
    return (
        coef[at, 0][None] * after
        + coef[at, 1][None] * before
        + coef[at, 2][None] * pltpu.roll(center, wide - 1, 2)
        + coef[at, 3][None] * pltpu.roll(center, 1, 2)
        + (coef[at, 4] - THETA[k] / SCALE)[None] * center
    )


def keep(pieces, at, k, value):
    cols = pieces.shape[-1]
    hi, lo = split(value[:, :, :cols].reshape(16, cols))
    pieces[at, HI_AT[k] : HI_AT[k] + 16, :] = hi
    pieces[at, LO_AT[k] : LO_AT[k] + 16, :] = lo


def add_gram(acc, rows):
    acc[...] += lax.dot_general(rows, rows, (((1,), (1,)), ((), ())), preferred_element_type=F32)


def middle_kernel(own, side, basis, first, second, third, acc, v1, v2, v3, coef, pieces, sems):
    tile_rows = own.shape[0]
    levels = (None, v1, v2, v3)
    acc[...] = jnp.zeros_like(acc)
    copies = []

    def start(source, target):
        copy = pltpu.make_async_copy(source, target, sems.at[len(copies)])
        copy.start()
        copies.append(copy)

    def get(k, r):
        if k:
            return levels[k][r]
        return jnp.concatenate([own[r], side[r]], axis=2)

    for front in range(1, tile_rows + 1):
        if front < tile_rows - 1:
            coefficients(coef, front, get(0, front))
        for k in range(S):
            r = front - k
            if k < r < tile_rows - 1 - k:
                value = newton_row(coef, r, k, get(k, r), get(k, r + 1), get(k, r - 1))
                if k < S - 1:
                    levels[k + 1][r] = value
                    group, at = (first, second, third)[k], export_at(k + 1, r, tile_rows)
                    if at is not None:
                        start(levels[k + 1].at[r], group.at[at])
                if HALO <= r < tile_rows - HALO:
                    keep(pieces, r - HALO, k + 1, value)
                    if k == 0:
                        keep(pieces, r - HALO, 0, get(0, r))
        r = front - S
        if HALO <= r < tile_rows - HALO:
            add_gram(acc, pieces[r - HALO])
            start(pieces.at[r - HALO, 0:128, :], basis.at[r - HALO])
    for copy in copies:
        copy.wait()


def export_at(k, r, tile_rows):
    low = {1: (1, 2, 3), 2: (2, 3), 3: (3, 4)}[k]
    rows = low + tuple(tile_rows - 1 - i for i in reversed(low))
    return rows.index(r) if r in rows else None


def edge_kernel(
    core, own, side, near, across, first, second, third, middle, pick, basis, payload, v1, v2, v3, coef, pieces, acc, sems
):
    tile_rows = own.shape[0]
    levels = (None, v1, v2, v3)
    exports = (None, first, second, third)
    acc[...] = middle[...]
    even = core[0] == 0
    copies = []

    def get(k, r):
        if k:
            at = export_at(k, r, tile_rows)
            return levels[k][r + HALO] if at is None else exports[k][at]
        if r < 0:
            return jnp.where(even, across[r + HALO], near[r + HALO])
        if r >= tile_rows:
            return jnp.where(even, near[r - tile_rows], across[r - tile_rows])
        return jnp.concatenate([own[r], side[r]], axis=2)

    def finish(at):
        add_gram(acc, pieces[at])
        copy = pltpu.make_async_copy(pieces.at[at, 0:128, :], basis.at[at], sems.at[at])
        copy.start()
        copies.append(copy)

    ready = []
    for far in (False, True):
        def place(i):
            return tile_rows - 1 - i if far else i

        def slot(i):
            return i + HALO if far else i

        for i in range(1 - HALO, HALO):
            coefficients(coef, place(i) + HALO, get(0, place(i)))
        for k in range(S):
            for i in range(k + 1 - HALO, k + 1):
                r = place(i)
                value = newton_row(coef, r + HALO, k, get(k, r), get(k, r + 1), get(k, r - 1))
                if k < S - 1:
                    levels[k + 1][r + HALO] = value
                if i >= 0:
                    keep(pieces, slot(i), k + 1, value)
                if k == S - 1:
                    ready.append(slot(i))
                if ready and (far or k == S - 1) and i % 2 == 1:
                    finish(ready.pop(0))
            for i in range(k + 1, HALO):
                if k < S - 1:
                    keep(pieces, slot(i), k + 1, get(k + 1, place(i)))
            if k == 0:
                for i in range(HALO):
                    keep(pieces, slot(i), 0, get(0, place(i)))
    for at in ready:
        finish(at)

    half = jnp.dot(pick[0:64, :], acc[...], precision=HIGH, preferred_element_type=F32)
    gram = lax.dot_general(half, pick[...], (((1,), (1,)), ((), ())), precision=HIGH, preferred_element_type=F32)
    row = lax.broadcasted_iota(jnp.int32, (32, 128), 0)
    column = lax.broadcasted_iota(jnp.int32, (32, 128), 1)
    one, two = gram[0:32], gram[32:64]
    cross = pltpu.roll(one, 96, 1)
    shifted = pltpu.roll(one, 32, 1)
    diagonal = jnp.sum(jnp.where(column == row + 32, two, 0.0), axis=1, keepdims=True)
    packed = jnp.where(row + 32 >= column, shifted, two)
    packed = jnp.where(column == 63, jnp.broadcast_to(diagonal, (32, 128)), packed)
    whole = jnp.where(column < 32, cross, packed)
    whole = jnp.where(column < 64, whole, 0.0)
    folded = whole[0:16] + pltpu.roll(whole[16:32], 64, 1)
    payload[...] = jnp.broadcast_to(folded[None], payload.shape)
    for copy in copies:
        copy.wait()


def gather_rows(right_side, diffusion, drift_field, strips, sems, at):
    tile_rows = diffusion.shape[0]
    first, second = CH * tile_rows, (CH + 1) * tile_rows
    cols = pl.ds(at[1] * LANE, LANE)
    copies = (
        (right_side.at[:, cols], strips.at[at[0], 0:first]),
        (diffusion.at[:, cols], strips.at[at[0], first:second]),
        (drift_field.at[:, cols], strips.at[at[0], second : second + 2 * tile_rows]),
    )
    copies = [pltpu.make_async_copy(a, b, sems.at[at[0], i]) for i, (a, b) in enumerate(copies)]
    for copy in copies:
        copy.start()
    return copies


def edges_kernel(right_side, diffusion, drift_field, left, right, strips, sems):
    tile_rows, tile_cols = diffusion.shape
    outs = (left, right)
    places = (0, tile_cols // LANE - 1)
    copies = [gather_rows(right_side, diffusion, drift_field, strips, sems, (i, p)) for i, p in enumerate(places)]
    for i in range(2):
        strips[i, 15 * tile_rows :] = jnp.zeros((tile_rows, LANE), F32)
        for copy in copies[i]:
            copy.wait()
        for r in range(tile_rows):
            for half in range(2):
                outs[i][r, half] = strips.at[i][pl.ds(8 * half * tile_rows + r, 8, stride=tile_rows), :]


def fields_kernel(right_side, diffusion, drift_field, fields, strips, sems):
    tile_rows, tile_cols = diffusion.shape
    count = tile_cols // LANE
    copies = [gather_rows(right_side, diffusion, drift_field, strips, sems, (i, i)) for i in range(count)]
    for i in range(count):
        strips[i, 15 * tile_rows :] = jnp.zeros((tile_rows, LANE), F32)
        for copy in copies[i]:
            copy.wait()
        for r in range(tile_rows):
            for half in range(2):
                fields[r, half, :, i * LANE : (i + 1) * LANE] = strips.at[i][
                    pl.ds(8 * half * tile_rows + r, 8, stride=tile_rows), :
                ]


def lane(shape):
    return lax.broadcasted_iota(jnp.int32, shape, len(shape) - 1)


def unpack(parts):
    total = parts[0]
    for i in range(1, parts.shape[0]):
        total = total + parts[i]
    row = lax.broadcasted_iota(jnp.int32, (32, 128), 0)
    column = lax.broadcasted_iota(jnp.int32, (32, 128), 1)
    whole = jnp.concatenate([total, pltpu.roll(total, 64, 1)], axis=0)
    whole = jnp.where(column < 64, whole, 0.0)
    flipped = jnp.concatenate([whole, jnp.zeros((96, 128), F32)], axis=0).T
    packed = pltpu.roll(whole, 96, 1)
    turned = flipped[32:64]
    diagonal = jnp.broadcast_to(whole[:, 63:64], (32, 128))
    first = jnp.where(row >= column, packed, turned)
    second = jnp.where(row < column, packed, turned)
    second = jnp.where(row == column, diagonal, second)
    left = column < 32
    top = jnp.where(left, first, pltpu.roll(whole, 32, 1))
    bottom = jnp.where(left, flipped[0:32], pltpu.roll(second, 32, 1))
    gram = jnp.concatenate([top, bottom], axis=0)
    gram = jnp.where(lane((64, 128)) < 30, gram, pltpu.roll(gram, 126, 1))
    return jnp.where(lax.broadcasted_iota(jnp.int32, (64, 128), 0) < 30, gram, pltpu.roll(gram, 62, 0))


def normal_systems(g, shifts):
    lanes = lane((48, 128))
    rows_id = lax.broadcasted_iota(jnp.int32, (48, 128), 0)
    theta_col = jnp.zeros((48, 128), F32)
    theta_row = jnp.zeros((48, 128), F32)
    for k in range(S):
        theta_row = jnp.where((rows_id >= 12 * k) & (rows_id < 12 * k + 12), THETA[k], theta_row)
        theta_col = jnp.where((lanes >= 12 * k) & (lanes < 12 * k + 12), THETA[k], theta_col)
    g0 = g[0:48]
    gd = pltpu.roll(g, 64 - 12, 0)[0:48]
    gr = pltpu.roll(g0, 128 - 12, 1)
    grd = pltpu.roll(gd, 128 - 12, 1)
    inside = lanes < 48
    at_rhs = lanes == 48
    systems = []
    for j in range(CH // 2):
        a = shifts[0, j]
        b = shifts[1, j]
        alpha_i = theta_row - a
        alpha_l = theta_col - a
        real = (alpha_i * alpha_l + b * b) * g0 + SCALE * (alpha_i * gr + alpha_l * gd) + SCALE * SCALE * grd
        imag = b * ((alpha_l - alpha_i) * g0 + SCALE * (gr - gd))
        g1 = pltpu.roll(g0, 48 - 2 * j, 1)
        g2 = pltpu.roll(g0, 47 - 2 * j, 1)
        gd1 = pltpu.roll(gd, 48 - 2 * j, 1)
        gd2 = pltpu.roll(gd, 47 - 2 * j, 1)
        rhs_real = alpha_i * g1 - b * g2 + SCALE * gd1
        rhs_imag = alpha_i * g2 + b * g1 + SCALE * gd2
        real = jnp.where(inside, real, jnp.where(at_rhs, rhs_real, 0.0))
        imag = jnp.where(inside, imag, jnp.where(at_rhs, rhs_imag, 0.0))
        systems.append((real, imag))
    left = lanes < 64
    pairs = []
    for first, second in zip(systems[::2], systems[1::2]):
        both = [jnp.where(left, f, pltpu.roll(g, 64, 1)) for f, g in zip(first, second)]
        pairs.append([[part[8 * i : 8 * i + 8] for i in range(6)] for part in both])
    return pairs


def eliminate(pairs):
    lanes = lane((8, 128))
    rows_id = lax.broadcasted_iota(jnp.int32, (8, 128), 0)
    for k in range(0, 48, 2):
        at, p = k // 8, k % 8
        where = jnp.where(lanes < 64, k, 64 + k)
        for pair in pairs:
            columns = [
                [jnp.take_along_axis(part[i], where + n, axis=1) for part in pair] for n in range(2) for i in range(6)
            ]
            (a, _), (zr, zi), (d, _) = columns[at], columns[6 + at], columns[6 + at]
            a, zr, zi, d = a[p : p + 1], zr[p : p + 1], zi[p : p + 1], d[p + 1 : p + 2]
            scale = 1.0 / (a * d - (zr * zr + zi * zi))
            a, zr, zi, d = a * scale, zr * scale, zi * scale, d * scale
            r0, i0, r1, i1 = (pair[part][at][p + n : p + n + 1] for n in range(2) for part in range(2))
            xr0 = d * r0 - (zr * r1 - zi * i1)
            xi0 = d * i0 - (zr * i1 + zi * r1)
            xr1 = a * r1 - (zr * r0 + zi * i0)
            xi1 = a * i1 - (zr * i0 - zi * r0)
            for i in range(6):
                (cr0, ci0), (cr1, ci1) = columns[i], columns[6 + i]
                real = pair[0][i] - ((cr0 * xr0 - ci0 * xi0) + (cr1 * xr1 - ci1 * xi1))
                imag = pair[1][i] - ((cr0 * xi0 + ci0 * xr0) + (cr1 * xi1 + ci1 * xr1))
                if i == at:
                    real = jnp.where(rows_id == p, xr0, jnp.where(rows_id == p + 1, xr1, real))
                    imag = jnp.where(rows_id == p, xi0, jnp.where(rows_id == p + 1, xi1, imag))
                pair[0][i], pair[1][i] = real, imag
    return pairs


def solve_kernel(shifts, parts, spread, middle_hbm, edge_hbm, out, middle, edge, mixed, sems):
    tile_rows = middle.shape[0] + edge.shape[0]
    strips = mixed.shape[0]
    copies = [
        pltpu.make_async_copy(middle_hbm, middle, sems.at[0]),
        pltpu.make_async_copy(edge_hbm, edge, sems.at[1]),
    ]
    for copy in copies:
        copy.start()

    pairs = eliminate(normal_systems(unpack(parts), shifts))
    lanes = lane((48, 128))
    mix = jnp.zeros((48, 128), F32)
    for q, pair in enumerate(pairs):
        for n, part in enumerate(pair):
            m = jnp.concatenate(part, axis=0)
            for side in range(2):
                at = 48 + 64 * side
                mix = jnp.where(lanes == 4 * q + 2 * side + n, jnp.broadcast_to(m[:, at : at + 1], (48, 128)), mix)
    mix = jnp.dot(spread[...], mix, precision=HIGH, preferred_element_type=F32)
    mix_hi, mix_lo = split(mix)
    weights = mix_hi.astype(F32) + pltpu.roll(mix_lo.astype(F32), 16, 1)
    weights = jnp.concatenate([weights, weights], axis=0).T[0:32].astype(BF16)

    for copy in copies:
        copy.wait()

    def combine(pieces, r):
        both = jnp.dot(weights, pieces, preferred_element_type=F32)
        both = both[0:16] + both[16:32]
        for j in range(strips):
            mixed.at[j][pl.ds(r, CH, stride=tile_rows), :] = both[0:CH, j * LANE : (j + 1) * LANE]

    for i in range(tile_rows - 2 * HALO):
        combine(middle[i], i + HALO)
    for i in range(HALO):
        combine(edge[i], i)
        combine(edge[i + HALO], tile_rows - 1 - i)
    copies = [
        pltpu.make_async_copy(mixed.at[j], out.at[:, j * LANE : (j + 1) * LANE], sems.at[2 + j]) for j in range(strips)
    ]
    for copy in copies:
        copy.start()
    for copy in copies:
        copy.wait()


def per_device(right_side, diffusion, drift_field, shifts):
    tile_rows, tile_cols = right_side.shape[1:]
    wide, mid_rows, depth = tile_cols + LANE, tile_rows - 2 * HALO, tile_rows + 2 * HALO
    anywhere = pl.BlockSpec(memory_space=pl.ANY)
    vmem = pl.BlockSpec(memory_space=pltpu.VMEM)
    far = pl.BlockSpec(memory_space=pltpu.HBM)
    scalar = pl.BlockSpec(memory_space=pltpu.SMEM)

    def params(mib):
        return pltpu.CompilerParams(vmem_limit_bytes=mib * 2**20)

    count = tile_cols // LANE

    def rows_of(n, width=wide):
        return (n, 2, 8, width)

    raw = (
        right_side.reshape(CH * tile_rows, tile_cols),
        diffusion,
        drift_field.reshape(2 * tile_rows, tile_cols),
    )
    left, right = pl.pallas_call(
        edges_kernel,
        out_shape=[jax.ShapeDtypeStruct(rows_of(tile_rows, LANE), F32)] * 2,
        in_specs=[anywhere] * 3,
        scratch_shapes=[pltpu.VMEM((2, 16 * tile_rows, LANE), F32), pltpu.SemaphoreType.DMA((2, 3))],
        compiler_params=params(60),
        name="edges",
    )(*raw)
    gy = lax.axis_size("x")
    from_left = lax.ppermute(right, "x", [(i, i + 1) for i in range(gy - 1)])
    from_right = lax.ppermute(left, "x", [(i + 1, i) for i in range(gy - 1)])
    side = jnp.where(lax.broadcasted_iota(jnp.int32, from_left.shape, 3) < LANE // 2, from_right, from_left)
    fields = pl.pallas_call(
        fields_kernel,
        out_shape=jax.ShapeDtypeStruct(rows_of(tile_rows, tile_cols), F32),
        in_specs=[anywhere] * 3,
        scratch_shapes=[pltpu.VMEM((count, 16 * tile_rows, LANE), F32), pltpu.SemaphoreType.DMA((count, 3))],
        compiler_params=params(60),
        cost_estimate=pl.CostEstimate(flops=10**6, bytes_accessed=4 * 10**6, transcendentals=0),
        name="fields",
    )(*raw)
    core = lax.axis_index("core")
    start = jnp.concatenate([fields[:HALO], side[:HALO]], axis=3)
    end = jnp.concatenate([fields[-HALO:], side[-HALO:]], axis=3)
    gx = ("z", "y", "core")
    ring = lax.axis_size(gx)
    across = lax.ppermute(
        jnp.where(core == 0, start, end), gx, [(i, (i + 2 * (i % 2) - 1) % ring) for i in range(ring)]
    )
    near = lax.ppermute(jnp.where(core == 0, end, start), "core", [(0, 1), (1, 0)])
    middle, first, second, third, partial = pl.pallas_call(
        middle_kernel,
        out_shape=(
            jax.ShapeDtypeStruct((mid_rows, 128, tile_cols), BF16),
            jax.ShapeDtypeStruct(rows_of(6), F32),
            jax.ShapeDtypeStruct(rows_of(4), F32),
            jax.ShapeDtypeStruct(rows_of(4), F32),
            jax.ShapeDtypeStruct((ROWS, ROWS), F32),
        ),
        in_specs=[vmem, vmem],
        out_specs=(far, anywhere, anywhere, anywhere, vmem),
        scratch_shapes=[
            *[pltpu.VMEM(rows_of(tile_rows), F32) for _ in range(3)],
            pltpu.VMEM((tile_rows, 5, 8, wide), F32),
            pltpu.VMEM((mid_rows, ROWS, tile_cols), BF16),
            pltpu.SemaphoreType.DMA((14 + mid_rows,)),
        ],
        compiler_params=params(60),
        cost_estimate=pl.CostEstimate(flops=10**9, bytes_accessed=20 * 10**6, transcendentals=0),
        name="middle",
    )(fields, side)
    edge, payload = pl.pallas_call(
        edge_kernel,
        out_shape=(
            jax.ShapeDtypeStruct((2 * HALO, 128, tile_cols), BF16),
            jax.ShapeDtypeStruct((32, 16, LANE), F32),
        ),
        in_specs=[scalar, *[vmem] * 9],
        out_specs=(far, vmem),
        scratch_shapes=[
            *[pltpu.VMEM(rows_of(depth), F32) for _ in range(3)],
            pltpu.VMEM((depth, 5, 8, wide), F32),
            pltpu.VMEM((2 * HALO, ROWS, tile_cols), BF16),
            pltpu.VMEM((ROWS, ROWS), F32),
            pltpu.SemaphoreType.DMA((2 * HALO,)),
        ],
        compiler_params=params(60),
        name="edge",
    )(core.reshape(1), fields, side, near, across, first, second, third, partial, jnp.asarray(selection()))

    parts = lax.all_to_all(payload, ("y", "core", "x"), 0, 0, tiled=True)
    total = jnp.sum(parts, axis=0)
    parts = lax.all_to_all(
        jnp.broadcast_to(total[None], (lax.axis_size("z"), 16, LANE)), ("z",), 0, 0, tiled=True
    )

    out = pl.pallas_call(
        solve_kernel,
        out_shape=jax.ShapeDtypeStruct((CH * tile_rows, tile_cols), F32),
        in_specs=[scalar, vmem, vmem, far, far],
        out_specs=anywhere,
        scratch_shapes=[
            pltpu.VMEM((mid_rows, 128, tile_cols), BF16),
            pltpu.VMEM((2 * HALO, 128, tile_cols), BF16),
            pltpu.VMEM((tile_cols // LANE, CH * tile_rows, LANE), F32),
            pltpu.SemaphoreType.DMA((2 + tile_cols // LANE,)),
        ],
        compiler_params=params(60),
        name="solve",
    )(shifts.T, parts, jnp.asarray(expansion()), middle, edge)
    return out.reshape(CH, tile_rows, tile_cols)


def solution(mesh):
    fine = Mesh(mesh.devices.reshape(16, 4, 2, 4), ("z", "y", "core", "x"))
    gx = ("z", "y", "core")
    in_specs = (P(None, gx, "x"), P(gx, "x"), P(None, gx, "x"), P())
    return jax.shard_map(
        per_device, mesh=fine, in_specs=in_specs, out_specs=P(None, gx, "x"), check_vma=False
    )
```

```python
import jax
import jax.numpy as jnp
import numpy as np
from jax import lax
from jax.experimental import pallas as pl
from jax.experimental.pallas import tpu as pltpu
from jax.sharding import Mesh
from jax.sharding import PartitionSpec as P

S = 4
THETA = (-8.0, -2.0, -14.0, -5.0)
SCALE = 8.0
CH = 12
HALO = 4
LANE = 128
HIGH = lax.Precision.HIGHEST
F32 = jnp.float32
BF16 = jnp.bfloat16
HI_AT = (0, 16, 32, 48, 128)
LO_AT = (64, 80, 96, 112, 144)
ROWS = 160


def selection():
    pick = np.zeros((128, ROWS), np.float32)
    for k in range(S + 1):
        for c in range(CH):
            i = k * CH + c
            at = i if i < 30 else i + 2
            pick[at, HI_AT[k] + c] = 1.0
            pick[at, LO_AT[k] + c] = 1.0
    return pick


def expansion():
    spread = np.zeros((64, 48), np.float32)
    for k in range(S):
        for c in range(CH):
            spread[k * 16 + c, k * CH + c] = 1.0
    return spread


def split(value):
    high = value.astype(BF16)
    return high, (value - high.astype(F32)).astype(BF16)


def coefficients(coef, at, field):
    shape = (8, field.shape[-1])
    spread = jnp.broadcast_to(field[1, 4:5, :], shape) * (1.0 / SCALE)
    drift_x = jnp.broadcast_to(field[1, 5:6, :], shape) * (0.5 / SCALE)
    drift_y = jnp.broadcast_to(field[1, 6:7, :], shape) * (0.5 / SCALE)
    coef[at, 0] = spread + drift_x
    coef[at, 1] = spread - drift_x
    coef[at, 2] = spread + drift_y
    coef[at, 3] = spread - drift_y
    coef[at, 4] = -4.0 * spread


def newton_row(coef, at, k, center, after, before):
    wide = center.shape[-1]
    return (
        coef[at, 0][None] * after
        + coef[at, 1][None] * before
        + coef[at, 2][None] * pltpu.roll(center, wide - 1, 2)
        + coef[at, 3][None] * pltpu.roll(center, 1, 2)
        + (coef[at, 4] - THETA[k] / SCALE)[None] * center
    )


def keep(pieces, at, k, value):
    cols = pieces.shape[-1]
    hi, lo = split(value[:, :, :cols].reshape(16, cols))
    pieces[at, HI_AT[k] : HI_AT[k] + 16, :] = hi
    pieces[at, LO_AT[k] : LO_AT[k] + 16, :] = lo


def add_gram(acc, rows):
    acc[...] += lax.dot_general(rows, rows, (((1,), (1,)), ((), ())), preferred_element_type=F32)


def middle_kernel(own, side, basis, first, second, third, acc, v1, v2, v3, coef, pieces, sems):
    tile_rows = own.shape[0]
    levels = (None, v1, v2, v3)
    acc[...] = jnp.zeros_like(acc)
    copies = []

    def start(source, target):
        copy = pltpu.make_async_copy(source, target, sems.at[len(copies)])
        copy.start()
        copies.append(copy)

    def get(k, r):
        if k:
            return levels[k][r]
        return jnp.concatenate([own[r], side[r]], axis=2)

    for front in range(1, tile_rows + 1):
        if front < tile_rows - 1:
            coefficients(coef, front, get(0, front))
        for k in range(S):
            r = front - k
            if k < r < tile_rows - 1 - k:
                value = newton_row(coef, r, k, get(k, r), get(k, r + 1), get(k, r - 1))
                if k < S - 1:
                    levels[k + 1][r] = value
                    group, at = (first, second, third)[k], export_at(k + 1, r, tile_rows)
                    if at is not None:
                        start(levels[k + 1].at[r], group.at[at])
                if HALO <= r < tile_rows - HALO:
                    keep(pieces, r - HALO, k + 1, value)
                    if k == 0:
                        keep(pieces, r - HALO, 0, get(0, r))
        r = front - S
        if HALO <= r < tile_rows - HALO:
            add_gram(acc, pieces[r - HALO])
            start(pieces.at[r - HALO, 0:128, :], basis.at[r - HALO])
    for copy in copies:
        copy.wait()


def export_at(k, r, tile_rows):
    low = {1: (1, 2, 3), 2: (2, 3), 3: (3, 4)}[k]
    rows = low + tuple(tile_rows - 1 - i for i in reversed(low))
    return rows.index(r) if r in rows else None


def edge_kernel(
    core, own, side, near, across, first, second, third, middle, pick, basis, payload, v1, v2, v3, coef, pieces, acc, sems
):
    tile_rows = own.shape[0]
    levels = (None, v1, v2, v3)
    exports = (None, first, second, third)
    acc[...] = middle[...]
    even = core[0] == 0
    copies = []

    def get(k, r):
        if k:
            at = export_at(k, r, tile_rows)
            return levels[k][r + HALO] if at is None else exports[k][at]
        if r < 0:
            return jnp.where(even, across[r + HALO], near[r + HALO])
        if r >= tile_rows:
            return jnp.where(even, near[r - tile_rows], across[r - tile_rows])
        return jnp.concatenate([own[r], side[r]], axis=2)

    def finish(at):
        add_gram(acc, pieces[at])
        copy = pltpu.make_async_copy(pieces.at[at, 0:128, :], basis.at[at], sems.at[at])
        copy.start()
        copies.append(copy)

    ready = []
    for far in (False, True):
        def place(i):
            return tile_rows - 1 - i if far else i

        def slot(i):
            return i + HALO if far else i

        for i in range(1 - HALO, HALO):
            coefficients(coef, place(i) + HALO, get(0, place(i)))
        for k in range(S):
            for i in range(k + 1 - HALO, k + 1):
                r = place(i)
                value = newton_row(coef, r + HALO, k, get(k, r), get(k, r + 1), get(k, r - 1))
                if k < S - 1:
                    levels[k + 1][r + HALO] = value
                if i >= 0:
                    keep(pieces, slot(i), k + 1, value)
                if k == S - 1:
                    ready.append(slot(i))
                if ready and (far or k == S - 1) and i % 2 == 1:
                    finish(ready.pop(0))
            for i in range(k + 1, HALO):
                if k < S - 1:
                    keep(pieces, slot(i), k + 1, get(k + 1, place(i)))
            if k == 0:
                for i in range(HALO):
                    keep(pieces, slot(i), 0, get(0, place(i)))
    for at in ready:
        finish(at)

    half = jnp.dot(pick[0:64, :], acc[...], precision=HIGH, preferred_element_type=F32)
    gram = lax.dot_general(half, pick[...], (((1,), (1,)), ((), ())), precision=HIGH, preferred_element_type=F32)
    row = lax.broadcasted_iota(jnp.int32, (32, 128), 0)
    column = lax.broadcasted_iota(jnp.int32, (32, 128), 1)
    one, two = gram[0:32], gram[32:64]
    cross = pltpu.roll(one, 96, 1)
    shifted = pltpu.roll(one, 32, 1)
    diagonal = jnp.sum(jnp.where(column == row + 32, two, 0.0), axis=1, keepdims=True)
    packed = jnp.where(row + 32 >= column, shifted, two)
    packed = jnp.where(column == 63, jnp.broadcast_to(diagonal, (32, 128)), packed)
    whole = jnp.where(column < 32, cross, packed)
    whole = jnp.where(column < 64, whole, 0.0)
    folded = whole[0:16] + pltpu.roll(whole[16:32], 64, 1)
    payload[...] = jnp.broadcast_to(folded[None], payload.shape)
    for copy in copies:
        copy.wait()


def gather_rows(right_side, diffusion, drift_field, strips, sems, at):
    tile_rows = diffusion.shape[0]
    first, second = CH * tile_rows, (CH + 1) * tile_rows
    cols = pl.ds(at[1] * LANE, LANE)
    copies = (
        (right_side.at[:, cols], strips.at[at[0], 0:first]),
        (diffusion.at[:, cols], strips.at[at[0], first:second]),
        (drift_field.at[:, cols], strips.at[at[0], second : second + 2 * tile_rows]),
    )
    copies = [pltpu.make_async_copy(a, b, sems.at[at[0], i]) for i, (a, b) in enumerate(copies)]
    for copy in copies:
        copy.start()
    return copies


def edges_kernel(place, right_side, diffusion, drift_field, inner, outer, strips, sems):
    tile_rows, tile_cols = diffusion.shape
    even = lax.rem(place[0], 2) == 0
    places = (0, tile_cols // LANE - 1)
    copies = [gather_rows(right_side, diffusion, drift_field, strips, sems, (i, p)) for i, p in enumerate(places)]
    for i in range(2):
        strips[i, 15 * tile_rows :] = jnp.zeros((tile_rows, LANE), F32)
        for copy in copies[i]:
            copy.wait()
    for r in range(tile_rows):
        for half in range(2):
            rows = pl.ds(8 * half * tile_rows + r, 8, stride=tile_rows)
            first, last = strips.at[0][rows, :], strips.at[1][rows, :]
            inner[r, half] = jnp.where(even, last, first)
            outer[r, half] = jnp.where(even, first, last)


def fields_kernel(right_side, diffusion, drift_field, fields, strips, turned, sems, out_sems):
    tile_rows, tile_cols = diffusion.shape
    count = tile_cols // LANE
    copies = [gather_rows(right_side, diffusion, drift_field, strips, sems, (i, i)) for i in range(count)]
    finished = []
    for i in range(count):
        strips[i, 15 * tile_rows :] = jnp.zeros((tile_rows, LANE), F32)
        for copy in copies[i]:
            copy.wait()
        for r in range(tile_rows):
            for half in range(2):
                turned[i, r, half] = strips.at[i][pl.ds(8 * half * tile_rows + r, 8, stride=tile_rows), :]
        copy = pltpu.make_async_copy(turned.at[i], fields.at[:, :, :, pl.ds(i * LANE, LANE)], out_sems.at[i])
        copy.start()
        finished.append(copy)
    for copy in finished:
        copy.wait()


def lane(shape):
    return lax.broadcasted_iota(jnp.int32, shape, len(shape) - 1)


def unpack(parts):
    total = parts[0]
    for i in range(1, parts.shape[0]):
        total = total + parts[i]
    row = lax.broadcasted_iota(jnp.int32, (32, 128), 0)
    column = lax.broadcasted_iota(jnp.int32, (32, 128), 1)
    whole = jnp.concatenate([total, pltpu.roll(total, 64, 1)], axis=0)
    whole = jnp.where(column < 64, whole, 0.0)
    flipped = jnp.concatenate([whole, jnp.zeros((96, 128), F32)], axis=0).T
    packed = pltpu.roll(whole, 96, 1)
    turned = flipped[32:64]
    diagonal = jnp.broadcast_to(whole[:, 63:64], (32, 128))
    first = jnp.where(row >= column, packed, turned)
    second = jnp.where(row < column, packed, turned)
    second = jnp.where(row == column, diagonal, second)
    left = column < 32
    top = jnp.where(left, first, pltpu.roll(whole, 32, 1))
    bottom = jnp.where(left, flipped[0:32], pltpu.roll(second, 32, 1))
    gram = jnp.concatenate([top, bottom], axis=0)
    gram = jnp.where(lane((64, 128)) < 30, gram, pltpu.roll(gram, 126, 1))
    return jnp.where(lax.broadcasted_iota(jnp.int32, (64, 128), 0) < 30, gram, pltpu.roll(gram, 62, 0))


def normal_systems(g, shifts):
    lanes = lane((48, 128))
    rows_id = lax.broadcasted_iota(jnp.int32, (48, 128), 0)
    theta_col = jnp.zeros((48, 128), F32)
    theta_row = jnp.zeros((48, 128), F32)
    for k in range(S):
        theta_row = jnp.where((rows_id >= 12 * k) & (rows_id < 12 * k + 12), THETA[k], theta_row)
        theta_col = jnp.where((lanes >= 12 * k) & (lanes < 12 * k + 12), THETA[k], theta_col)
    g0 = g[0:48]
    gd = pltpu.roll(g, 64 - 12, 0)[0:48]
    gr = pltpu.roll(g0, 128 - 12, 1)
    grd = pltpu.roll(gd, 128 - 12, 1)
    inside = lanes < 48
    at_rhs = lanes == 48
    systems = []
    for j in range(CH // 2):
        a = shifts[0, j]
        b = shifts[1, j]
        alpha_i = theta_row - a
        alpha_l = theta_col - a
        real = (alpha_i * alpha_l + b * b) * g0 + SCALE * (alpha_i * gr + alpha_l * gd) + SCALE * SCALE * grd
        imag = b * ((alpha_l - alpha_i) * g0 + SCALE * (gr - gd))
        g1 = pltpu.roll(g0, 48 - 2 * j, 1)
        g2 = pltpu.roll(g0, 47 - 2 * j, 1)
        gd1 = pltpu.roll(gd, 48 - 2 * j, 1)
        gd2 = pltpu.roll(gd, 47 - 2 * j, 1)
        rhs_real = alpha_i * g1 - b * g2 + SCALE * gd1
        rhs_imag = alpha_i * g2 + b * g1 + SCALE * gd2
        real = jnp.where(inside, real, jnp.where(at_rhs, rhs_real, 0.0))
        imag = jnp.where(inside, imag, jnp.where(at_rhs, rhs_imag, 0.0))
        systems.append((real, imag))
    left = lanes < 64
    pairs = []
    for first, second in zip(systems[::2], systems[1::2]):
        both = [jnp.where(left, f, pltpu.roll(g, 64, 1)) for f, g in zip(first, second)]
        pairs.append([[part[8 * i : 8 * i + 8] for i in range(6)] for part in both])
    return pairs


def eliminate(pairs):
    lanes = lane((8, 128))
    rows_id = lax.broadcasted_iota(jnp.int32, (8, 128), 0)
    for k in range(0, 48, 2):
        at, p = k // 8, k % 8
        where = jnp.where(lanes < 64, k, 64 + k)
        for pair in pairs:
            columns = [
                [jnp.take_along_axis(part[i], where + n, axis=1) for part in pair] for n in range(2) for i in range(6)
            ]
            (a, _), (zr, zi), (d, _) = columns[at], columns[6 + at], columns[6 + at]
            a, zr, zi, d = a[p : p + 1], zr[p : p + 1], zi[p : p + 1], d[p + 1 : p + 2]
            scale = 1.0 / (a * d - (zr * zr + zi * zi))
            a, zr, zi, d = a * scale, zr * scale, zi * scale, d * scale
            r0, i0, r1, i1 = (pair[part][at][p + n : p + n + 1] for n in range(2) for part in range(2))
            xr0 = d * r0 - (zr * r1 - zi * i1)
            xi0 = d * i0 - (zr * i1 + zi * r1)
            xr1 = a * r1 - (zr * r0 + zi * i0)
            xi1 = a * i1 - (zr * i0 - zi * r0)
            for i in range(6):
                (cr0, ci0), (cr1, ci1) = columns[i], columns[6 + i]
                real = pair[0][i] - ((cr0 * xr0 - ci0 * xi0) + (cr1 * xr1 - ci1 * xi1))
                imag = pair[1][i] - ((cr0 * xi0 + ci0 * xr0) + (cr1 * xi1 + ci1 * xr1))
                if i == at:
                    real = jnp.where(rows_id == p, xr0, jnp.where(rows_id == p + 1, xr1, real))
                    imag = jnp.where(rows_id == p, xi0, jnp.where(rows_id == p + 1, xi1, imag))
                pair[0][i], pair[1][i] = real, imag
    return pairs


def solve_kernel(shifts, parts, spread, middle_hbm, edge_hbm, out, middle, edge, mixed, sems):
    tile_rows = middle.shape[0] + edge.shape[0]
    strips = mixed.shape[0]
    copies = [
        pltpu.make_async_copy(middle_hbm, middle, sems.at[0]),
        pltpu.make_async_copy(edge_hbm, edge, sems.at[1]),
    ]
    for copy in copies:
        copy.start()

    pairs = eliminate(normal_systems(unpack(parts), shifts))
    lanes = lane((48, 128))
    mix = jnp.zeros((48, 128), F32)
    for q, pair in enumerate(pairs):
        for n, part in enumerate(pair):
            m = jnp.concatenate(part, axis=0)
            for side in range(2):
                at = 48 + 64 * side
                mix = jnp.where(lanes == 4 * q + 2 * side + n, jnp.broadcast_to(m[:, at : at + 1], (48, 128)), mix)
    mix = jnp.dot(spread[...], mix, precision=HIGH, preferred_element_type=F32)
    mix_hi, mix_lo = split(mix)
    weights = mix_hi.astype(F32) + pltpu.roll(mix_lo.astype(F32), 16, 1)
    weights = jnp.concatenate([weights, weights], axis=0).T[0:32].astype(BF16)

    for copy in copies:
        copy.wait()

    def combine(pieces, r):
        both = jnp.dot(weights, pieces, preferred_element_type=F32)
        both = both[0:16] + both[16:32]
        for j in range(strips):
            mixed.at[j][pl.ds(r, CH, stride=tile_rows), :] = both[0:CH, j * LANE : (j + 1) * LANE]

    for i in range(tile_rows - 2 * HALO):
        combine(middle[i], i + HALO)
    for i in range(HALO):
        combine(edge[i], i)
        combine(edge[i + HALO], tile_rows - 1 - i)
    copies = [
        pltpu.make_async_copy(mixed.at[j], out.at[:, j * LANE : (j + 1) * LANE], sems.at[2 + j]) for j in range(strips)
    ]
    for copy in copies:
        copy.start()
    for copy in copies:
        copy.wait()


def per_device(right_side, diffusion, drift_field, shifts):
    tile_rows, tile_cols = right_side.shape[1:]
    wide, mid_rows, depth = tile_cols + LANE, tile_rows - 2 * HALO, tile_rows + 2 * HALO
    anywhere = pl.BlockSpec(memory_space=pl.ANY)
    vmem = pl.BlockSpec(memory_space=pltpu.VMEM)
    far = pl.BlockSpec(memory_space=pltpu.HBM)
    scalar = pl.BlockSpec(memory_space=pltpu.SMEM)

    def params(mib):
        return pltpu.CompilerParams(vmem_limit_bytes=mib * 2**20)

    count = tile_cols // LANE

    def rows_of(n, width=wide):
        return (n, 2, 8, width)

    raw = (
        right_side.reshape(CH * tile_rows, tile_cols),
        diffusion,
        drift_field.reshape(2 * tile_rows, tile_cols),
    )
    place = lax.axis_index("x")
    inner, outer = pl.pallas_call(
        edges_kernel,
        out_shape=[jax.ShapeDtypeStruct(rows_of(tile_rows, LANE), F32)] * 2,
        in_specs=[scalar, *[anywhere] * 3],
        scratch_shapes=[pltpu.VMEM((2, 16 * tile_rows, LANE), F32), pltpu.SemaphoreType.DMA((2, 3))],
        compiler_params=params(60),
        name="edges",
    )(place.reshape(1), *raw)
    gy = lax.axis_size("x")
    inner = lax.ppermute(inner, "x", [(i, i ^ 1) for i in range(gy)])
    outer = lax.ppermute(outer, "x", [(i, i + 2 * (i % 2) - 1) for i in range(1, gy - 1)])
    after = lax.broadcasted_iota(jnp.int32, inner.shape, 3) < LANE // 2
    side = jnp.where(after == (place % 2 == 0), inner, outer)
    fields = pl.pallas_call(
        fields_kernel,
        out_shape=jax.ShapeDtypeStruct(rows_of(tile_rows, tile_cols), F32),
        in_specs=[anywhere] * 3,
        out_specs=far,
        scratch_shapes=[
            pltpu.VMEM((count, 16 * tile_rows, LANE), F32),
            pltpu.VMEM((count, *rows_of(tile_rows, LANE)), F32),
            pltpu.SemaphoreType.DMA((count, 3)),
            pltpu.SemaphoreType.DMA((count,)),
        ],
        compiler_params=params(60),
        cost_estimate=pl.CostEstimate(flops=10**6, bytes_accessed=4 * 10**6, transcendentals=0),
        name="fields",
    )(*raw)
    core = lax.axis_index("core")
    start = jnp.concatenate([fields[:HALO], side[:HALO]], axis=3)
    end = jnp.concatenate([fields[-HALO:], side[-HALO:]], axis=3)
    gx = ("z", "y", "core")
    ring = lax.axis_size(gx)
    across = lax.ppermute(
        jnp.where(core == 0, start, end), gx, [(i, (i + 2 * (i % 2) - 1) % ring) for i in range(ring)]
    )
    near = lax.ppermute(jnp.where(core == 0, end, start), "core", [(0, 1), (1, 0)])
    middle, first, second, third, partial = pl.pallas_call(
        middle_kernel,
        out_shape=(
            jax.ShapeDtypeStruct((mid_rows, 128, tile_cols), BF16),
            jax.ShapeDtypeStruct(rows_of(6), F32),
            jax.ShapeDtypeStruct(rows_of(4), F32),
            jax.ShapeDtypeStruct(rows_of(4), F32),
            jax.ShapeDtypeStruct((ROWS, ROWS), F32),
        ),
        in_specs=[vmem, vmem],
        out_specs=(far, anywhere, anywhere, anywhere, vmem),
        scratch_shapes=[
            *[pltpu.VMEM(rows_of(tile_rows), F32) for _ in range(3)],
            pltpu.VMEM((tile_rows, 5, 8, wide), F32),
            pltpu.VMEM((mid_rows, ROWS, tile_cols), BF16),
            pltpu.SemaphoreType.DMA((14 + mid_rows,)),
        ],
        compiler_params=params(60),
        cost_estimate=pl.CostEstimate(flops=10**9, bytes_accessed=20 * 10**6, transcendentals=0),
        name="middle",
    )(fields, side)
    edge, payload = pl.pallas_call(
        edge_kernel,
        out_shape=(
            jax.ShapeDtypeStruct((2 * HALO, 128, tile_cols), BF16),
            jax.ShapeDtypeStruct((32, 16, LANE), F32),
        ),
        in_specs=[scalar, *[vmem] * 9],
        out_specs=(far, vmem),
        scratch_shapes=[
            *[pltpu.VMEM(rows_of(depth), F32) for _ in range(3)],
            pltpu.VMEM((depth, 5, 8, wide), F32),
            pltpu.VMEM((2 * HALO, ROWS, tile_cols), BF16),
            pltpu.VMEM((ROWS, ROWS), F32),
            pltpu.SemaphoreType.DMA((2 * HALO,)),
        ],
        compiler_params=params(60),
        name="edge",
    )(core.reshape(1), fields, side, near, across, first, second, third, partial, jnp.asarray(selection()))

    parts = lax.all_to_all(payload, ("y", "core", "x"), 0, 0, tiled=True)
    total = jnp.sum(parts, axis=0)
    parts = lax.all_to_all(
        jnp.broadcast_to(total[None], (lax.axis_size("z"), 16, LANE)), ("z",), 0, 0, tiled=True
    )

    out = pl.pallas_call(
        solve_kernel,
        out_shape=jax.ShapeDtypeStruct((CH * tile_rows, tile_cols), F32),
        in_specs=[scalar, vmem, vmem, far, far],
        out_specs=anywhere,
        scratch_shapes=[
            pltpu.VMEM((mid_rows, 128, tile_cols), BF16),
            pltpu.VMEM((2 * HALO, 128, tile_cols), BF16),
            pltpu.VMEM((tile_cols // LANE, CH * tile_rows, LANE), F32),
            pltpu.SemaphoreType.DMA((2 + tile_cols // LANE,)),
        ],
        compiler_params=params(60),
        name="solve",
    )(shifts.T, parts, jnp.asarray(expansion()), middle, edge)
    return out.reshape(CH, tile_rows, tile_cols)


def solution(mesh):
    fine = Mesh(mesh.devices.reshape(16, 4, 2, 4), ("z", "y", "core", "x"))
    gx = ("z", "y", "core")
    in_specs = (P(None, gx, "x"), P(gx, "x"), P(None, gx, "x"), P())
    return jax.shard_map(
        per_device, mesh=fine, in_specs=in_specs, out_specs=P(None, gx, "x"), check_vma=False
    )
```

```python
import jax
import jax.numpy as jnp
import numpy as np
from jax import lax
from jax.experimental import pallas as pl
from jax.experimental.pallas import tpu as pltpu
from jax.sharding import Mesh
from jax.sharding import PartitionSpec as P

S = 4
THETA = (-8.0, -2.0, -14.0, -5.0)
SCALE = 8.0
CH = 12
HALO = 4
LANE = 128
HIGH = lax.Precision.HIGHEST
F32 = jnp.float32
BF16 = jnp.bfloat16
HI_AT = (0, 16, 32, 48, 128)
LO_AT = (64, 80, 96, 112, 144)
ROWS = 160


def selection():
    pick = np.zeros((128, ROWS), np.float32)
    for k in range(S + 1):
        for c in range(CH):
            i = k * CH + c
            at = i if i < 30 else i + 2
            pick[at, HI_AT[k] + c] = 1.0
            pick[at, LO_AT[k] + c] = 1.0
    return pick


def expansion():
    spread = np.zeros((64, 48), np.float32)
    for k in range(S):
        for c in range(CH):
            spread[k * 16 + c, k * CH + c] = 1.0
    return spread


def split(value):
    high = value.astype(BF16)
    return high, (value - high.astype(F32)).astype(BF16)


def coefficients(coef, at, field):
    shape = (8, field.shape[-1])
    spread = jnp.broadcast_to(field[1, 4:5, :], shape) * (1.0 / SCALE)
    drift_x = jnp.broadcast_to(field[1, 5:6, :], shape) * (0.5 / SCALE)
    drift_y = jnp.broadcast_to(field[1, 6:7, :], shape) * (0.5 / SCALE)
    coef[at, 0] = spread + drift_x
    coef[at, 1] = spread - drift_x
    coef[at, 2] = spread + drift_y
    coef[at, 3] = spread - drift_y
    coef[at, 4] = -4.0 * spread


def newton_row(coef, at, k, center, after, before):
    wide = center.shape[-1]
    return (
        coef[at, 0][None] * after
        + coef[at, 1][None] * before
        + coef[at, 2][None] * pltpu.roll(center, wide - 1, 2)
        + coef[at, 3][None] * pltpu.roll(center, 1, 2)
        + (coef[at, 4] - THETA[k] / SCALE)[None] * center
    )


def keep(pieces, at, k, value):
    cols = pieces.shape[-1]
    hi, lo = split(value[:, :, :cols].reshape(16, cols))
    pieces[at, HI_AT[k] : HI_AT[k] + 16, :] = hi
    pieces[at, LO_AT[k] : LO_AT[k] + 16, :] = lo


def add_gram(acc, rows):
    acc[...] += lax.dot_general(rows, rows, (((1,), (1,)), ((), ())), preferred_element_type=F32)


def middle_kernel(own, side, basis, first, second, third, acc, v1, v2, v3, coef, pieces, sems):
    tile_rows = own.shape[0]
    levels = (None, v1, v2, v3)
    acc[...] = jnp.zeros_like(acc)
    copies = []

    def start(source, target):
        copy = pltpu.make_async_copy(source, target, sems.at[len(copies)])
        copy.start()
        copies.append(copy)

    def get(k, r):
        if k:
            return levels[k][r]
        return jnp.concatenate([own[r], side[r]], axis=2)

    for front in range(1, tile_rows + 1):
        if front < tile_rows - 1:
            coefficients(coef, front, get(0, front))
        for k in range(S):
            r = front - k
            if k < r < tile_rows - 1 - k:
                value = newton_row(coef, r, k, get(k, r), get(k, r + 1), get(k, r - 1))
                if k < S - 1:
                    levels[k + 1][r] = value
                    group, at = (first, second, third)[k], export_at(k + 1, r, tile_rows)
                    if at is not None:
                        start(levels[k + 1].at[r], group.at[at])
                if HALO <= r < tile_rows - HALO:
                    keep(pieces, r - HALO, k + 1, value)
                    if k == 0:
                        keep(pieces, r - HALO, 0, get(0, r))
        r = front - S
        if HALO <= r < tile_rows - HALO:
            add_gram(acc, pieces[r - HALO])
            start(pieces.at[r - HALO, 0:128, :], basis.at[r - HALO])
    for copy in copies:
        copy.wait()


def export_at(k, r, tile_rows):
    low = {1: (1, 2, 3), 2: (2, 3), 3: (3, 4)}[k]
    rows = low + tuple(tile_rows - 1 - i for i in reversed(low))
    return rows.index(r) if r in rows else None


def edge_kernel(
    core, own, side, near, across, first, second, third, middle, pick, basis, payload, v1, v2, v3, coef, pieces, acc, sems
):
    tile_rows = own.shape[0]
    levels = (None, v1, v2, v3)
    exports = (None, first, second, third)
    acc[...] = middle[...]
    even = core[0] == 0
    copies = []

    def get(k, r):
        if k:
            at = export_at(k, r, tile_rows)
            return levels[k][r + HALO] if at is None else exports[k][at]
        if r < 0:
            return jnp.where(even, across[r + HALO], near[r + HALO])
        if r >= tile_rows:
            return jnp.where(even, near[r - tile_rows], across[r - tile_rows])
        return jnp.concatenate([own[r], side[r]], axis=2)

    def finish(at):
        add_gram(acc, pieces[at])
        copy = pltpu.make_async_copy(pieces.at[at, 0:128, :], basis.at[at], sems.at[at])
        copy.start()
        copies.append(copy)

    ready = []
    for far in (False, True):
        def place(i):
            return tile_rows - 1 - i if far else i

        def slot(i):
            return i + HALO if far else i

        for i in range(1 - HALO, HALO):
            coefficients(coef, place(i) + HALO, get(0, place(i)))
        for k in range(S):
            for i in range(k + 1 - HALO, k + 1):
                r = place(i)
                value = newton_row(coef, r + HALO, k, get(k, r), get(k, r + 1), get(k, r - 1))
                if k < S - 1:
                    levels[k + 1][r + HALO] = value
                if i >= 0:
                    keep(pieces, slot(i), k + 1, value)
                if k == S - 1:
                    ready.append(slot(i))
                if ready and (far or k == S - 1) and i % 2 == 1:
                    finish(ready.pop(0))
            for i in range(k + 1, HALO):
                if k < S - 1:
                    keep(pieces, slot(i), k + 1, get(k + 1, place(i)))
            if k == 0:
                for i in range(HALO):
                    keep(pieces, slot(i), 0, get(0, place(i)))
    for at in ready:
        finish(at)

    half = jnp.dot(pick[0:64, :], acc[...], precision=HIGH, preferred_element_type=F32)
    gram = lax.dot_general(half, pick[...], (((1,), (1,)), ((), ())), precision=HIGH, preferred_element_type=F32)
    row = lax.broadcasted_iota(jnp.int32, (32, 128), 0)
    column = lax.broadcasted_iota(jnp.int32, (32, 128), 1)
    one, two = gram[0:32], gram[32:64]
    cross = pltpu.roll(one, 96, 1)
    shifted = pltpu.roll(one, 32, 1)
    diagonal = jnp.sum(jnp.where(column == row + 32, two, 0.0), axis=1, keepdims=True)
    packed = jnp.where(row + 32 >= column, shifted, two)
    packed = jnp.where(column == 63, jnp.broadcast_to(diagonal, (32, 128)), packed)
    whole = jnp.where(column < 32, cross, packed)
    whole = jnp.where(column < 64, whole, 0.0)
    folded = whole[0:16] + pltpu.roll(whole[16:32], 64, 1)
    payload[...] = folded
    for copy in copies:
        copy.wait()


def gather_rows(right_side, diffusion, drift_field, strips, sems, at):
    tile_rows = diffusion.shape[0]
    first, second = CH * tile_rows, (CH + 1) * tile_rows
    cols = pl.ds(at[1] * LANE, LANE)
    copies = (
        (right_side.at[:, cols], strips.at[at[0], 0:first]),
        (diffusion.at[:, cols], strips.at[at[0], first:second]),
        (drift_field.at[:, cols], strips.at[at[0], second : second + 2 * tile_rows]),
    )
    copies = [pltpu.make_async_copy(a, b, sems.at[at[0], i]) for i, (a, b) in enumerate(copies)]
    for copy in copies:
        copy.start()
    return copies


def edges_kernel(place, right_side, diffusion, drift_field, inner, outer, strips, sems):
    tile_rows, tile_cols = diffusion.shape
    even = lax.rem(place[0], 2) == 0
    places = (0, tile_cols // LANE - 1)
    copies = [gather_rows(right_side, diffusion, drift_field, strips, sems, (i, p)) for i, p in enumerate(places)]
    for i in range(2):
        strips[i, 15 * tile_rows :] = jnp.zeros((tile_rows, LANE), F32)
        for copy in copies[i]:
            copy.wait()
    for r in range(tile_rows):
        for half in range(2):
            rows = pl.ds(8 * half * tile_rows + r, 8, stride=tile_rows)
            first, last = strips.at[0][rows, :], strips.at[1][rows, :]
            inner[r, half] = jnp.where(even, last, first)
            outer[r, half] = jnp.where(even, first, last)


def fields_kernel(right_side, diffusion, drift_field, fields, strips, turned, sems, out_sems):
    tile_rows, tile_cols = diffusion.shape
    count = tile_cols // LANE
    copies = [gather_rows(right_side, diffusion, drift_field, strips, sems, (i, i)) for i in range(count)]
    finished = []
    for i in range(count):
        strips[i, 15 * tile_rows :] = jnp.zeros((tile_rows, LANE), F32)
        for copy in copies[i]:
            copy.wait()
        for r in range(tile_rows):
            for half in range(2):
                turned[i, r, half] = strips.at[i][pl.ds(8 * half * tile_rows + r, 8, stride=tile_rows), :]
        copy = pltpu.make_async_copy(turned.at[i], fields.at[:, :, :, pl.ds(i * LANE, LANE)], out_sems.at[i])
        copy.start()
        finished.append(copy)
    for copy in finished:
        copy.wait()


def lane(shape):
    return lax.broadcasted_iota(jnp.int32, shape, len(shape) - 1)


def unpack(parts):
    total = parts[0]
    for i in range(1, parts.shape[0]):
        total = total + parts[i]
    row = lax.broadcasted_iota(jnp.int32, (32, 128), 0)
    column = lax.broadcasted_iota(jnp.int32, (32, 128), 1)
    whole = jnp.concatenate([total, pltpu.roll(total, 64, 1)], axis=0)
    whole = jnp.where(column < 64, whole, 0.0)
    flipped = jnp.concatenate([whole, jnp.zeros((96, 128), F32)], axis=0).T
    packed = pltpu.roll(whole, 96, 1)
    turned = flipped[32:64]
    diagonal = jnp.broadcast_to(whole[:, 63:64], (32, 128))
    first = jnp.where(row >= column, packed, turned)
    second = jnp.where(row < column, packed, turned)
    second = jnp.where(row == column, diagonal, second)
    left = column < 32
    top = jnp.where(left, first, pltpu.roll(whole, 32, 1))
    bottom = jnp.where(left, flipped[0:32], pltpu.roll(second, 32, 1))
    gram = jnp.concatenate([top, bottom], axis=0)
    gram = jnp.where(lane((64, 128)) < 30, gram, pltpu.roll(gram, 126, 1))
    return jnp.where(lax.broadcasted_iota(jnp.int32, (64, 128), 0) < 30, gram, pltpu.roll(gram, 62, 0))


def normal_systems(g, shifts):
    lanes = lane((48, 128))
    rows_id = lax.broadcasted_iota(jnp.int32, (48, 128), 0)
    theta_col = jnp.zeros((48, 128), F32)
    theta_row = jnp.zeros((48, 128), F32)
    for k in range(S):
        theta_row = jnp.where((rows_id >= 12 * k) & (rows_id < 12 * k + 12), THETA[k], theta_row)
        theta_col = jnp.where((lanes >= 12 * k) & (lanes < 12 * k + 12), THETA[k], theta_col)
    g0 = g[0:48]
    gd = pltpu.roll(g, 64 - 12, 0)[0:48]
    gr = pltpu.roll(g0, 128 - 12, 1)
    grd = pltpu.roll(gd, 128 - 12, 1)
    inside = lanes < 48
    at_rhs = lanes == 48
    systems = []
    for j in range(CH // 2):
        a = shifts[0, j]
        b = shifts[1, j]
        alpha_i = theta_row - a
        alpha_l = theta_col - a
        real = (alpha_i * alpha_l + b * b) * g0 + SCALE * (alpha_i * gr + alpha_l * gd) + SCALE * SCALE * grd
        imag = b * ((alpha_l - alpha_i) * g0 + SCALE * (gr - gd))
        g1 = pltpu.roll(g0, 48 - 2 * j, 1)
        g2 = pltpu.roll(g0, 47 - 2 * j, 1)
        gd1 = pltpu.roll(gd, 48 - 2 * j, 1)
        gd2 = pltpu.roll(gd, 47 - 2 * j, 1)
        rhs_real = alpha_i * g1 - b * g2 + SCALE * gd1
        rhs_imag = alpha_i * g2 + b * g1 + SCALE * gd2
        real = jnp.where(inside, real, jnp.where(at_rhs, rhs_real, 0.0))
        imag = jnp.where(inside, imag, jnp.where(at_rhs, rhs_imag, 0.0))
        systems.append((real, imag))
    left = lanes < 64
    pairs = []
    for first, second in zip(systems[::2], systems[1::2]):
        both = [jnp.where(left, f, pltpu.roll(g, 64, 1)) for f, g in zip(first, second)]
        pairs.append([[part[8 * i : 8 * i + 8] for i in range(6)] for part in both])
    return pairs


def eliminate(pairs):
    lanes = lane((8, 128))
    rows_id = lax.broadcasted_iota(jnp.int32, (8, 128), 0)
    for k in range(0, 48, 2):
        at, p = k // 8, k % 8
        where = jnp.where(lanes < 64, k, 64 + k)
        for pair in pairs:
            columns = [
                [jnp.take_along_axis(part[i], where + n, axis=1) for part in pair] for n in range(2) for i in range(6)
            ]
            (a, _), (zr, zi), (d, _) = columns[at], columns[6 + at], columns[6 + at]
            a, zr, zi, d = a[p : p + 1], zr[p : p + 1], zi[p : p + 1], d[p + 1 : p + 2]
            scale = 1.0 / (a * d - (zr * zr + zi * zi))
            a, zr, zi, d = a * scale, zr * scale, zi * scale, d * scale
            r0, i0, r1, i1 = (pair[part][at][p + n : p + n + 1] for n in range(2) for part in range(2))
            xr0 = d * r0 - (zr * r1 - zi * i1)
            xi0 = d * i0 - (zr * i1 + zi * r1)
            xr1 = a * r1 - (zr * r0 + zi * i0)
            xi1 = a * i1 - (zr * i0 - zi * r0)
            for i in range(6):
                (cr0, ci0), (cr1, ci1) = columns[i], columns[6 + i]
                real = pair[0][i] - ((cr0 * xr0 - ci0 * xi0) + (cr1 * xr1 - ci1 * xi1))
                imag = pair[1][i] - ((cr0 * xi0 + ci0 * xr0) + (cr1 * xi1 + ci1 * xr1))
                if i == at:
                    real = jnp.where(rows_id == p, xr0, jnp.where(rows_id == p + 1, xr1, real))
                    imag = jnp.where(rows_id == p, xi0, jnp.where(rows_id == p + 1, xi1, imag))
                pair[0][i], pair[1][i] = real, imag
    return pairs


def solve_kernel(shifts, parts, spread, middle_hbm, edge_hbm, out, middle, edge, mixed, sems):
    tile_rows = middle.shape[0] + edge.shape[0]
    strips = mixed.shape[0]
    copies = [
        pltpu.make_async_copy(middle_hbm, middle, sems.at[0]),
        pltpu.make_async_copy(edge_hbm, edge, sems.at[1]),
    ]
    for copy in copies:
        copy.start()

    pairs = eliminate(normal_systems(unpack(parts), shifts))
    lanes = lane((48, 128))
    mix = jnp.zeros((48, 128), F32)
    for q, pair in enumerate(pairs):
        for n, part in enumerate(pair):
            m = jnp.concatenate(part, axis=0)
            for side in range(2):
                at = 48 + 64 * side
                mix = jnp.where(lanes == 4 * q + 2 * side + n, jnp.broadcast_to(m[:, at : at + 1], (48, 128)), mix)
    mix = jnp.dot(spread[...], mix, precision=HIGH, preferred_element_type=F32)
    mix_hi, mix_lo = split(mix)
    weights = mix_hi.astype(F32) + pltpu.roll(mix_lo.astype(F32), 16, 1)
    weights = jnp.concatenate([weights, weights], axis=0).T[0:32].astype(BF16)

    for copy in copies:
        copy.wait()

    def combine(pieces, r):
        both = jnp.dot(weights, pieces, preferred_element_type=F32)
        both = both[0:16] + both[16:32]
        for j in range(strips):
            mixed.at[j][pl.ds(r, CH, stride=tile_rows), :] = both[0:CH, j * LANE : (j + 1) * LANE]

    for i in range(tile_rows - 2 * HALO):
        combine(middle[i], i + HALO)
    for i in range(HALO):
        combine(edge[i], i)
        combine(edge[i + HALO], tile_rows - 1 - i)
    copies = [
        pltpu.make_async_copy(mixed.at[j], out.at[:, j * LANE : (j + 1) * LANE], sems.at[2 + j]) for j in range(strips)
    ]
    for copy in copies:
        copy.start()
    for copy in copies:
        copy.wait()


def per_device(right_side, diffusion, drift_field, shifts):
    tile_rows, tile_cols = right_side.shape[1:]
    wide, mid_rows, depth = tile_cols + LANE, tile_rows - 2 * HALO, tile_rows + 2 * HALO
    anywhere = pl.BlockSpec(memory_space=pl.ANY)
    vmem = pl.BlockSpec(memory_space=pltpu.VMEM)
    far = pl.BlockSpec(memory_space=pltpu.HBM)
    scalar = pl.BlockSpec(memory_space=pltpu.SMEM)

    def params(mib):
        return pltpu.CompilerParams(vmem_limit_bytes=mib * 2**20)

    count = tile_cols // LANE

    def rows_of(n, width=wide):
        return (n, 2, 8, width)

    raw = (
        right_side.reshape(CH * tile_rows, tile_cols),
        diffusion,
        drift_field.reshape(2 * tile_rows, tile_cols),
    )
    place = lax.axis_index("x")
    inner, outer = pl.pallas_call(
        edges_kernel,
        out_shape=[jax.ShapeDtypeStruct(rows_of(tile_rows, LANE), F32)] * 2,
        in_specs=[scalar, *[anywhere] * 3],
        scratch_shapes=[pltpu.VMEM((2, 16 * tile_rows, LANE), F32), pltpu.SemaphoreType.DMA((2, 3))],
        compiler_params=params(60),
        name="edges",
    )(place.reshape(1), *raw)
    gy = lax.axis_size("x")
    inner = lax.ppermute(inner, "x", [(i, i ^ 1) for i in range(gy)])
    outer = lax.ppermute(outer, "x", [(i, i + 2 * (i % 2) - 1) for i in range(1, gy - 1)])
    after = lax.broadcasted_iota(jnp.int32, inner.shape, 3) < LANE // 2
    side = jnp.where(after == (place % 2 == 0), inner, outer)
    fields = pl.pallas_call(
        fields_kernel,
        out_shape=jax.ShapeDtypeStruct(rows_of(tile_rows, tile_cols), F32),
        in_specs=[anywhere] * 3,
        out_specs=far,
        scratch_shapes=[
            pltpu.VMEM((count, 16 * tile_rows, LANE), F32),
            pltpu.VMEM((count, *rows_of(tile_rows, LANE)), F32),
            pltpu.SemaphoreType.DMA((count, 3)),
            pltpu.SemaphoreType.DMA((count,)),
        ],
        compiler_params=params(60),
        cost_estimate=pl.CostEstimate(flops=10**6, bytes_accessed=4 * 10**6, transcendentals=0),
        name="fields",
    )(*raw)
    core = lax.axis_index("core")
    start = jnp.concatenate([fields[:HALO], side[:HALO]], axis=3)
    end = jnp.concatenate([fields[-HALO:], side[-HALO:]], axis=3)
    gx = ("z", "y", "core")
    ring = lax.axis_size(gx)
    across = lax.ppermute(
        jnp.where(core == 0, start, end), gx, [(i, (i + 2 * (i % 2) - 1) % ring) for i in range(ring)]
    )
    near = lax.ppermute(jnp.where(core == 0, end, start), "core", [(0, 1), (1, 0)])
    middle, first, second, third, partial = pl.pallas_call(
        middle_kernel,
        out_shape=(
            jax.ShapeDtypeStruct((mid_rows, 128, tile_cols), BF16),
            jax.ShapeDtypeStruct(rows_of(6), F32),
            jax.ShapeDtypeStruct(rows_of(4), F32),
            jax.ShapeDtypeStruct(rows_of(4), F32),
            jax.ShapeDtypeStruct((ROWS, ROWS), F32),
        ),
        in_specs=[vmem, vmem],
        out_specs=(far, anywhere, anywhere, anywhere, vmem),
        scratch_shapes=[
            *[pltpu.VMEM(rows_of(tile_rows), F32) for _ in range(3)],
            pltpu.VMEM((tile_rows, 5, 8, wide), F32),
            pltpu.VMEM((mid_rows, ROWS, tile_cols), BF16),
            pltpu.SemaphoreType.DMA((14 + mid_rows,)),
        ],
        compiler_params=params(60),
        cost_estimate=pl.CostEstimate(flops=10**9, bytes_accessed=20 * 10**6, transcendentals=0),
        name="middle",
    )(fields, side)
    edge, payload = pl.pallas_call(
        edge_kernel,
        out_shape=(
            jax.ShapeDtypeStruct((2 * HALO, 128, tile_cols), BF16),
            jax.ShapeDtypeStruct((16, LANE), F32),
        ),
        in_specs=[scalar, *[vmem] * 9],
        out_specs=(far, vmem),
        scratch_shapes=[
            *[pltpu.VMEM(rows_of(depth), F32) for _ in range(3)],
            pltpu.VMEM((depth, 5, 8, wide), F32),
            pltpu.VMEM((2 * HALO, ROWS, tile_cols), BF16),
            pltpu.VMEM((ROWS, ROWS), F32),
            pltpu.SemaphoreType.DMA((2 * HALO,)),
        ],
        compiler_params=params(60),
        name="edge",
    )(core.reshape(1), fields, side, near, across, first, second, third, partial, jnp.asarray(selection()))

    for axes in (("y", "core", "x"), ("z",)):
        copies = jnp.broadcast_to(payload[None], (lax.axis_size(axes), 16, LANE))
        parts = lax.all_to_all(copies, axes, 0, 0, tiled=True)
        payload = jnp.sum(parts, axis=0)

    middle, edge = (pltpu.with_memory_space_constraint(x, pltpu.HBM) for x in (middle, edge))
    out = pl.pallas_call(
        solve_kernel,
        out_shape=jax.ShapeDtypeStruct((CH * tile_rows, tile_cols), F32),
        in_specs=[scalar, vmem, vmem, far, far],
        out_specs=anywhere,
        scratch_shapes=[
            pltpu.VMEM((mid_rows, 128, tile_cols), BF16),
            pltpu.VMEM((2 * HALO, 128, tile_cols), BF16),
            pltpu.VMEM((tile_cols // LANE, CH * tile_rows, LANE), F32),
            pltpu.SemaphoreType.DMA((2 + tile_cols // LANE,)),
        ],
        compiler_params=params(16),
        name="solve",
    )(shifts.T, parts, jnp.asarray(expansion()), middle, edge)
    return out.reshape(CH, tile_rows, tile_cols)


def solution(mesh):
    fine = Mesh(mesh.devices.reshape(16, 4, 2, 4), ("z", "y", "core", "x"))
    gx = ("z", "y", "core")
    in_specs = (P(None, gx, "x"), P(gx, "x"), P(None, gx, "x"), P())
    return jax.shard_map(
        per_device, mesh=fine, in_specs=in_specs, out_specs=P(None, gx, "x"), check_vma=False
    )
```
